512 devices in a mesh: seq: 64 (over y, x, core), chan: 8 (over z).
Axes of the slice: x: 4, y: 8, z: 8, core: 2. Of those that a mesh axis runs over, the one named last changes fastest.
Arguments:
- inputs: bfloat16 [4096, 8192], P('chan', 'seq'), may hold values from -6 to 6
- grad_out: bfloat16 [4096, 8192], P('chan', 'seq'), may hold values from -0.0625 to 0.0625
- out_weight: float32 [4096, 64], P('chan'), may hold values from -0.75 to 0.75
- decay_rate: float32 [4096], P('chan'), may hold values from 6.1035156e-05 to 0.04
- frequency: float32 [64], replicated, may hold values from 0.00036621094 to 1.5
- phase_shift: float32 [64], replicated, may hold values from -3.140625 to 3.140625
- sketch_matrix: float32 [4096, 32], P('chan'), may hold values from -0.0014648438 to 0.0014648438
Outputs:
- grad_input: bfloat16 [4096, 8192], P('chan', 'seq')
- grad_filter: bfloat16 [4096, 8192], P('chan', 'seq')
- sketch: float32 [32, 64], replicated
The draws below stay inside these ranges and needn't reach their ends.
All inputs are finite; a program needn't handle non-finite values.
Results may differ from the reference program's by a relative error of at most 0.005.
Values may be sent and summed in bfloat16 or wider, within the bound.
No kernel may reach another device: no remote copies, remote signals or barrier semaphores. Data moves between devices by JAX's collectives and lax.ppermute only.
A program may use at most 64 MiB of HBM per device.

```python
import math
import jax
import jax.numpy as jnp
from jax import lax

WIDTH = 4096
ORDER = 64
RANK = 32
SEQ = 8192


def steps_of(stream_key, dims, split, low, largest):
    factor_of, own = 1.0, jax.random.fold_in(stream_key, 6)
    for axis_at, blocks in split:
        draws = jnp.exp(jax.random.uniform(jax.random.fold_in(own, axis_at), (blocks,), jnp.float32, low / len(split), largest / len(split)))
        factor_of = factor_of * jnp.repeat(draws, dims[axis_at] // blocks).reshape([-1 if axis == axis_at else 1 for axis in range(len(dims))])
    return factor_of


def bell_draw(rng, dims, scale, limit, split=(), dtype=jnp.bfloat16):
    drawn = jax.random.normal(rng, dims, jnp.float32) * scale
    if len(split) > 0:
        drawn = steps_of(rng, dims, split, -0.22, 0.18) * drawn
    return jnp.clip(drawn, min=-limit, max=limit).astype(dtype)


def setup_inputs(seed: int = 0) -> dict:
    key_list = jax.random.split(jax.random.key(seed), 8)
    return {
        "inputs": bell_draw(key_list[0], (WIDTH, SEQ), 1.0, 6.0, ((0, 8), (1, 64))),
        "grad_out": bell_draw(key_list[1], (WIDTH, SEQ), SEQ ** -0.5, 0.0625, ((0, 8), (1, 64))),
        "out_weight": bell_draw(key_list[2], (WIDTH, ORDER), ORDER ** -0.5, 0.75, ((0, 8),), jnp.float32),
        "decay_rate": jnp.clip(jnp.exp(math.log(0.04) - 6.4851847 * jax.random.uniform(key_list[3], (WIDTH,), jnp.float32) ** steps_of(key_list[3], (WIDTH,), ((0, 8),), -0.2, 0.2)), 6.103515625e-05, 0.04),
        "frequency": jnp.clip(jnp.exp(jax.random.uniform(key_list[4], (ORDER,), jnp.float32, math.log(0.00036621094), math.log(1.5))), 0.00036621094, 1.5),
        "phase_shift": jnp.clip(jax.random.uniform(key_list[5], (ORDER,), jnp.float32, -3.140625, 3.140625), -3.140625, 3.140625),
        "sketch_matrix": bell_draw(key_list[6], (WIDTH, RANK), (WIDTH * SEQ // 2) ** -0.5, 0.0014648438, ((0, 8),), jnp.float32),
    }


highest = lax.Precision.HIGHEST


def make_filter(weights, rates, basis, positions):
    mixed = jnp.dot(weights, basis, precision=highest, preferred_element_type=jnp.float32)
    return mixed * jnp.exp(-rates[:, None] * positions[None, :])


def reference(inputs, grad_out, out_weight, decay_rate, frequency, phase_shift, sketch_matrix):
    positions = jnp.arange(SEQ).astype(jnp.float32)
    basis = jnp.sin(frequency[:, None] * positions[None, :] + phase_shift[:, None])
    n_fft = 2 * SEQ
    block = min(256, WIDTH)
    count = WIDTH // block

    def one_block(pieces):
        sig_u, sig_g, weights, rates, sketch_rows = pieces
        envelope = jnp.exp(-rates[:, None] * positions[None, :])
        filt = (jnp.dot(weights, basis, precision=highest, preferred_element_type=jnp.float32) * envelope).astype(jnp.bfloat16)
        spec_u = jnp.fft.rfft(sig_u.astype(jnp.float32), n=n_fft, axis=1)
        spec_h = jnp.fft.rfft(filt.astype(jnp.float32), n=n_fft, axis=1)
        spec_g = jnp.fft.rfft(sig_g.astype(jnp.float32), n=n_fft, axis=1)
        grad_in = jnp.fft.irfft(spec_g * jnp.conj(spec_h), n=n_fft, axis=1)[:, :SEQ].astype(jnp.bfloat16)
        grad_h = jnp.fft.irfft(spec_g * jnp.conj(spec_u), n=n_fft, axis=1)[:, :SEQ].astype(jnp.bfloat16)
        grad_mix = jnp.dot(grad_h.astype(jnp.float32) * envelope, basis.T, precision=highest, preferred_element_type=jnp.float32)
        partial_sum = jnp.dot(sketch_rows.T, grad_mix, precision=highest, preferred_element_type=jnp.float32)
        return grad_in, grad_h, partial_sum

    grad_in, grad_h, partials = lax.map(one_block, (
        inputs.reshape(count, block, SEQ),
        grad_out.reshape(count, block, SEQ),
        out_weight.reshape(count, block, ORDER),
        decay_rate.reshape(count, block),
        sketch_matrix.reshape(count, block, RANK)))
    sketch = jnp.sum(partials, axis=0)
    return grad_in.reshape(WIDTH, SEQ), grad_h.reshape(WIDTH, SEQ), sketch
```

```python
import math

import jax
import jax.numpy as jnp
from jax import lax
from jax.experimental import pallas as pl
from jax.experimental.pallas import tpu as pltpu
from jax.sharding import PartitionSpec as P

LANES = 128
GROUP = 4

highest = lax.Precision.HIGHEST


def slab_kernel(got_ref, filt_ref, turn_ref, wave_ref, fall_ref, flip_ref, out_ref, rev_u, rev_f, rows_g, rows_o, mix):
    blocks = got_ref.shape[0]
    chans = filt_ref.shape[0]
    f32, bf16 = jnp.float32, jnp.bfloat16
    pad = rev_u.shape[0] // chans
    gpad = rows_g.shape[0] // chans
    flip = flip_ref[...]
    rev_u[...] = jnp.zeros(rev_u.shape, f32)
    rev_f[...] = jnp.zeros(rev_f.shape, f32)
    rows_g[...] = jnp.zeros(rows_g.shape, f32)
    for c in range(chans):
        rev_f[c * pad : c * pad + blocks, :] = filt_ref[c]
    for t in range(blocks):
        tile = got_ref[t]
        turned = jnp.dot(tile, flip, preferred_element_type=f32)
        rev_u[pl.ds(blocks - 1 - t, chans, stride=pad), :] = turned[:chans]
        rows_g[pl.ds(t, chans, stride=gpad), :] = tile.astype(f32)[chans:]

    row_id = lax.broadcasted_iota(jnp.int32, (LANES, LANES), 0)
    lane_id = lax.broadcasted_iota(jnp.int32, (LANES, LANES), 1)
    own = (lane_id <= row_id).astype(f32)

    def rolled(c, d):
        row = jnp.broadcast_to(rows_g[pl.ds(c * gpad + d, 1), :], (LANES, LANES))
        return pltpu.roll(row, 1, 1, stride=1, stride_axis=0)

    def channel(c, carry):
        acc = [[jnp.zeros((16, LANES), f32) for _ in range(blocks // 16)] for _ in range(2)]
        here = rolled(c, 0)
        for d0 in range(0, blocks, GROUP):
            pieces = []
            for d in range(d0, d0 + GROUP):
                after = rolled(c, d + 1)
                pieces.append(jnp.where(own > 0.5, here, after).astype(bf16))
                here = after
            hank = jnp.concatenate(pieces, axis=0)
            count = -(-(d0 + GROUP) // 16)
            left = []
            for ref in (rev_f, rev_u):
                left.append(
                    jnp.concatenate(
                        [
                            ref[pl.ds(c * pad + blocks - 1 - d, 16 * count), :].astype(bf16)
                            for d in range(d0, d0 + GROUP)
                        ],
                        axis=1,
                    )
                )
            res = jnp.dot(jnp.concatenate(left, axis=0), hank, preferred_element_type=f32)
            for s in range(2):
                for n in range(count):
                    at = (s * count + n) * 16
                    acc[s][n] = acc[s][n] + res[at : at + 16]
        grad_in = jnp.concatenate(acc[0], axis=0)
        grad_h = jnp.concatenate(acc[1], axis=0)
        rows_o[pl.ds(c, blocks, stride=2 * chans), :] = grad_in
        rows_o[pl.ds(c + chans, blocks, stride=2 * chans), :] = grad_h
        kept = grad_h.astype(bf16).astype(f32) * fall_ref[pl.ds(c, 1), :]
        spun = jnp.dot(kept, wave_ref[...], precision=highest, preferred_element_type=f32)
        mix[pl.ds(c, 1), :] = jnp.sum(spun * turn_ref[c], axis=0, keepdims=True)
        return carry

    lax.fori_loop(0, chans, channel, 0)
    total = mix[...]
    total = total + pltpu.roll(total, LANES // 2, 1)
    high = total.astype(bf16).astype(f32)
    lanes = lax.broadcasted_iota(jnp.int32, total.shape, 1)
    pair = jnp.where(lanes < LANES // 2, high, total - high).astype(bf16)
    for t in range(blocks):
        out_ref[t, : 2 * chans, :] = rows_o[2 * chans * t : 2 * chans * (t + 1), :].astype(bf16)
        out_ref[t, 2 * chans :, :] = pair


def run_slab(got, filt, turn, wave, fall, flip, interpret=False):
    blocks, rows, _ = got.shape
    chans = rows // 2
    f32 = jnp.float32
    return pl.pallas_call(
        slab_kernel,
        out_shape=jax.ShapeDtypeStruct((blocks, 3 * chans, LANES), jnp.bfloat16),
        scratch_shapes=[
            pltpu.VMEM((chans * 2 * blocks, LANES), f32),
            pltpu.VMEM((chans * 2 * blocks, LANES), f32),
            pltpu.VMEM((chans * (blocks + 8), LANES), f32),
            pltpu.VMEM((2 * chans * blocks, LANES), f32),
            pltpu.VMEM((chans, LANES), f32),
        ],
        compiler_params=pltpu.CompilerParams(vmem_limit_bytes=32 << 20),
        interpret=interpret,
    )(got, filt, turn, wave, fall, flip)


def filter_tables(weights, rates, frequency, phase_shift, blocks):
    hi = (LANES * jnp.arange(blocks)).astype(jnp.float32)
    lo = jnp.arange(LANES).astype(jnp.float32)
    outer = frequency[None, :] * hi[:, None] + phase_shift[None, :]
    inner = frequency[:, None] * lo[None, :]
    turn = jnp.concatenate([jnp.sin(outer), jnp.cos(outer)], axis=1)
    wave = jnp.concatenate([jnp.cos(inner), jnp.sin(inner)], axis=0)
    turn = jnp.exp(-rates[:, None] * hi[None, :])[:, :, None] * turn[None]
    fall = jnp.exp(-rates[:, None] * lo[None, :])
    both = jnp.concatenate([weights, weights], axis=1)
    mixed = jnp.einsum("ckj,jl->ckl", (turn * both[:, None, :])[:, ::-1], wave[:, ::-1], precision=highest)
    filt = mixed * fall[:, None, ::-1]
    return filt, turn, wave.T, fall


def per_device(inputs, grad_out, out_weight, decay_rate, frequency, phase_shift, sketch_matrix):
    groups = lax.axis_size("seq")
    parts = lax.axis_size("chan")
    seq_index = lax.axis_index("seq")
    width_local, tok_len = inputs.shape
    chans = width_local // groups
    order = frequency.shape[0]
    first_row = seq_index * chans
    sent = jnp.concatenate(
        [inputs.reshape(groups, chans, tok_len), grad_out.reshape(groups, chans, tok_len)], axis=1
    )
    got = lax.all_to_all(sent, "seq", split_axis=0, concat_axis=0, tiled=True)
    rates = lax.dynamic_slice_in_dim(decay_rate, first_row, chans, 0)
    weights = lax.dynamic_slice_in_dim(out_weight, first_row, chans, 0)
    filt, turn, wave, fall = filter_tables(weights, rates, frequency, phase_shift, groups)
    flip = jnp.eye(LANES, dtype=jnp.bfloat16)[::-1]
    back = run_slab(got, filt, turn, wave, fall, flip)
    home = lax.all_to_all(back, "seq", split_axis=0, concat_axis=0, tiled=True)
    pair = home[:, 2 * chans :, :].astype(jnp.float32)
    grad_mix = (pair[:, :, :order] + pair[:, :, order:]).reshape(width_local, order)
    partial_sum = jnp.dot(sketch_matrix.T, grad_mix, precision=highest, preferred_element_type=jnp.float32)
    everyone = jnp.broadcast_to(partial_sum[None], (parts, *partial_sum.shape))
    sketch = jnp.sum(lax.all_to_all(everyone, "chan", split_axis=0, concat_axis=0, tiled=True), axis=0)
    grad_in = home[:, :chans, :].reshape(width_local, tok_len)
    grad_h = home[:, chans : 2 * chans, :].reshape(width_local, tok_len)
    return (grad_in, grad_h, sketch)


def solution(mesh):
    placed = (
        P("chan", "seq"),
        P("chan", "seq"),
        P("chan", None),
        P("chan"),
        P(),
        P(),
        P("chan", None),
    )
    return jax.shard_map(
        per_device,
        mesh=mesh,
        in_specs=placed,
        out_specs=(P("chan", "seq"), P("chan", "seq"), P()),
        check_vma=False,
    )
```

```python
import math

import jax
import jax.numpy as jnp
from jax import lax
from jax.experimental import pallas as pl
from jax.experimental.pallas import tpu as pltpu
from jax.sharding import PartitionSpec as P

LANES = 128
GROUP = 4

highest = lax.Precision.HIGHEST


def slab_kernel(got_ref, filt_ref, turn_ref, wave_ref, fall_ref, flip_ref, out_ref, rev_u, rev_f, rows_g, rows_o, kept):
    blocks = got_ref.shape[0]
    chans = filt_ref.shape[0]
    f32, bf16 = jnp.float32, jnp.bfloat16
    pad = rev_u.shape[0] // chans
    gpad = rows_g.shape[0] // chans
    flip = flip_ref[...]
    rev_u[...] = jnp.zeros(rev_u.shape, f32)
    rev_f[...] = jnp.zeros(rev_f.shape, f32)
    rows_g[...] = jnp.zeros(rows_g.shape, f32)
    for c in range(chans):
        rev_f[c * pad : c * pad + blocks, :] = filt_ref[c]
    turned = jnp.dot(got_ref[...].reshape(blocks * 2 * chans, LANES), flip, preferred_element_type=f32)
    for t in range(blocks):
        tile = got_ref[t]
        rev_u[pl.ds(blocks - 1 - t, chans, stride=pad), :] = turned[2 * chans * t : 2 * chans * t + chans]
        rows_g[pl.ds(t, chans, stride=gpad), :] = tile.astype(f32)[chans:]

    row_id = lax.broadcasted_iota(jnp.int32, (LANES, LANES), 0)
    lane_id = lax.broadcasted_iota(jnp.int32, (LANES, LANES), 1)
    own = (lane_id <= row_id).astype(bf16) > 0.5

    def rolled(c, d):
        row = jnp.broadcast_to(rows_g[pl.ds(c * gpad + d, 1), :], (LANES, LANES))
        return pltpu.roll(row, 1, 1, stride=1, stride_axis=0).astype(bf16)

    def channel(c, carry):
        acc = [[jnp.zeros((16, LANES), f32) for _ in range(blocks // 16)] for _ in range(2)]
        here = rolled(c, 0)
        for d0 in range(0, blocks, GROUP):
            pieces = []
            for d in range(d0, d0 + GROUP):
                after = rolled(c, d + 1)
                pieces.append(jnp.where(own, here, after))
                here = after
            hank = jnp.concatenate(pieces, axis=0)
            count = -(-(d0 + GROUP) // 16)
            left = []
            for ref in (rev_f, rev_u):
                left.append(
                    jnp.concatenate(
                        [
                            ref[pl.ds(c * pad + blocks - 1 - d, 16 * count), :].astype(bf16)
                            for d in range(d0, d0 + GROUP)
                        ],
                        axis=1,
                    )
                )
            res = jnp.dot(jnp.concatenate(left, axis=0), hank, preferred_element_type=f32)
            for s in range(2):
                for n in range(count):
                    at = (s * count + n) * 16
                    acc[s][n] = acc[s][n] + res[at : at + 16]
        grad_in = jnp.concatenate(acc[0], axis=0)
        grad_h = jnp.concatenate(acc[1], axis=0)
        rows_o[pl.ds(c, blocks, stride=2 * chans), :] = grad_in
        rows_o[pl.ds(c + chans, blocks, stride=2 * chans), :] = grad_h
        kept[pl.ds(pl.multiple_of(c * blocks, blocks), blocks), :] = grad_h.astype(bf16).astype(f32) * fall_ref[pl.ds(c, 1), :]
        return carry

    lax.fori_loop(0, chans, channel, 0, unroll=True)
    spun = jnp.dot(kept[...], wave_ref[...], precision=highest, preferred_element_type=f32)
    spun = spun.reshape(chans, blocks, LANES) * turn_ref[...]
    total = jnp.sum(spun, axis=1)
    total = total + pltpu.roll(total, LANES // 2, 1)
    high = total.astype(bf16).astype(f32)
    lanes = lax.broadcasted_iota(jnp.int32, total.shape, 1)
    pair = jnp.where(lanes < LANES // 2, high, total - high).astype(bf16)
    for t in range(blocks):
        out_ref[t, : 2 * chans, :] = rows_o[2 * chans * t : 2 * chans * (t + 1), :].astype(bf16)
        out_ref[t, 2 * chans :, :] = pair


def run_slab(got, filt, turn, wave, fall, flip, interpret=False):
    blocks, rows, _ = got.shape
    chans = rows // 2
    f32 = jnp.float32
    return pl.pallas_call(
        slab_kernel,
        out_shape=jax.ShapeDtypeStruct((blocks, 3 * chans, LANES), jnp.bfloat16),
        scratch_shapes=[
            pltpu.VMEM((chans * 2 * blocks, LANES), f32),
            pltpu.VMEM((chans * 2 * blocks, LANES), f32),
            pltpu.VMEM((chans * (blocks + 8), LANES), f32),
            pltpu.VMEM((2 * chans * blocks, LANES), f32),
            pltpu.VMEM((chans * blocks, LANES), f32),
        ],
        compiler_params=pltpu.CompilerParams(vmem_limit_bytes=32 << 20),
        interpret=interpret,
    )(got, filt, turn, wave, fall, flip)


def filter_tables(weights, rates, frequency, phase_shift, blocks):
    hi = (LANES * jnp.arange(blocks)).astype(jnp.float32)
    lo = jnp.arange(LANES).astype(jnp.float32)
    outer = frequency[None, :] * hi[:, None] + phase_shift[None, :]
    inner = frequency[:, None] * lo[None, :]
    turn = jnp.concatenate([jnp.sin(outer), jnp.cos(outer)], axis=1)
    wave = jnp.concatenate([jnp.cos(inner), jnp.sin(inner)], axis=0)
    turn = jnp.exp(-rates[:, None] * hi[None, :])[:, :, None] * turn[None]
    fall = jnp.exp(-rates[:, None] * lo[None, :])
    both = jnp.concatenate([weights, weights], axis=1)
    mixed = jnp.einsum("ckj,jl->ckl", (turn * both[:, None, :])[:, ::-1], wave[:, ::-1], precision=highest)
    filt = mixed * fall[:, None, ::-1]
    return filt, turn, wave.T, fall


def pack_kernel(u_ref, g_ref, out_ref):
    chans = u_ref.shape[1]
    out_ref[:, :chans, :] = u_ref[...]
    out_ref[:, chans:, :] = g_ref[...]


def partial_kernel(home_ref, rows_ref, out_ref):
    groups, rows, lanes = home_ref.shape
    chans = rows // 3
    pair = home_ref[:, 2 * chans :, :].astype(jnp.float32).reshape(groups * chans, lanes)
    sums = jnp.dot(rows_ref[...], pair, precision=highest, preferred_element_type=jnp.float32)
    sums = sums + pltpu.roll(sums, lanes // 2, 1)
    half = sums.shape[0] // 2
    lane_id = lax.broadcasted_iota(jnp.int32, (half, lanes), 1)
    folded = jnp.where(lane_id < lanes // 2, sums[:half], sums[half:])
    for part in range(out_ref.shape[0] // half):
        out_ref[part * half : (part + 1) * half, :] = folded


def total_kernel(parts_ref, out_ref):
    half, lanes = out_ref.shape[0] // 2, parts_ref.shape[1]
    total = parts_ref[:half]
    for part in range(1, parts_ref.shape[0] // half):
        total = total + parts_ref[part * half : (part + 1) * half]
    out_ref[:half, :] = total[:, : lanes // 2]
    out_ref[half:, :] = total[:, lanes // 2 :]


def per_device(inputs, grad_out, out_weight, decay_rate, frequency, phase_shift, sketch_matrix):
    groups = lax.axis_size("seq")
    parts = lax.axis_size("chan")
    seq_index = lax.axis_index("seq")
    width_local, tok_len = inputs.shape
    chans = width_local // groups
    order = frequency.shape[0]
    rank = sketch_matrix.shape[1]
    f32 = jnp.float32
    first_row = seq_index * chans
    sent = pl.pallas_call(pack_kernel, out_shape=jax.ShapeDtypeStruct((groups, 2 * chans, tok_len), inputs.dtype))(
        inputs.reshape(groups, chans, tok_len), grad_out.reshape(groups, chans, tok_len)
    )
    got = lax.all_to_all(sent, "seq", split_axis=0, concat_axis=0, tiled=True)
    rates = lax.dynamic_slice_in_dim(decay_rate, first_row, chans, 0)
    weights = lax.dynamic_slice_in_dim(out_weight, first_row, chans, 0)
    filt, turn, wave, fall = filter_tables(weights, rates, frequency, phase_shift, groups)
    flip = jnp.eye(LANES, dtype=jnp.bfloat16)[::-1]
    back = run_slab(got, filt, turn, wave, fall, flip)
    home = lax.all_to_all(back, "seq", split_axis=0, concat_axis=0, tiled=True)
    everyone = pl.pallas_call(partial_kernel, out_shape=jax.ShapeDtypeStruct((parts * rank // 2, LANES), f32))(
        home, sketch_matrix.T
    )
    gathered = lax.all_to_all(everyone, "chan", split_axis=0, concat_axis=0, tiled=True)
    sketch = pl.pallas_call(total_kernel, out_shape=jax.ShapeDtypeStruct((rank, order), f32))(gathered)
    grad_in = home[:, :chans, :].reshape(width_local, tok_len)
    grad_h = home[:, chans : 2 * chans, :].reshape(width_local, tok_len)
    return (grad_in, grad_h, sketch)


def solution(mesh):
    placed = (
        P("chan", "seq"),
        P("chan", "seq"),
        P("chan", None),
        P("chan"),
        P(),
        P(),
        P("chan", None),
    )
    return jax.shard_map(
        per_device,
        mesh=mesh,
        in_specs=placed,
        out_specs=(P("chan", "seq"), P("chan", "seq"), P()),
        check_vma=False,
    )
```

```python
import math

import jax
import jax.numpy as jnp
from jax import lax
from jax.experimental import pallas as pl
from jax.experimental.pallas import tpu as pltpu
from jax.sharding import PartitionSpec as P

LANES = 128
GROUP = 4
CHUNKS = 4

highest = lax.Precision.HIGHEST


def slab_kernel(got_ref, filt_ref, turn_ref, wave_ref, fall_ref, flip_ref, out_ref, rev_u, rev_f, rows_g, rows_o, kept):
    blocks = got_ref.shape[0]
    chans = filt_ref.shape[0]
    f32, bf16 = jnp.float32, jnp.bfloat16
    pad = rev_u.shape[0] // chans
    gpad = rows_g.shape[0] // chans
    flip = flip_ref[...]
    rev_u[...] = jnp.zeros(rev_u.shape, f32)
    rev_f[...] = jnp.zeros(rev_f.shape, f32)
    rows_g[...] = jnp.zeros(rows_g.shape, f32)
    for c in range(chans):
        rev_f[c * pad : c * pad + blocks, :] = filt_ref[c]
    turned = jnp.dot(got_ref[...].reshape(blocks * 2 * chans, LANES), flip, preferred_element_type=f32)
    for t in range(blocks):
        tile = got_ref[t]
        rev_u[pl.ds(blocks - 1 - t, chans, stride=pad), :] = turned[2 * chans * t : 2 * chans * t + chans]
        rows_g[pl.ds(t, chans, stride=gpad), :] = tile.astype(f32)[chans:]

    row_id = lax.broadcasted_iota(jnp.int32, (LANES, LANES), 0)
    lane_id = lax.broadcasted_iota(jnp.int32, (LANES, LANES), 1)
    own = (lane_id <= row_id).astype(bf16) > 0.5

    def rolled(c, d):
        row = jnp.broadcast_to(rows_g[pl.ds(c * gpad + d, 1), :], (LANES, LANES))
        return pltpu.roll(row, 1, 1, stride=1, stride_axis=0).astype(bf16)

    def channel(c, carry):
        acc = [[jnp.zeros((16, LANES), f32) for _ in range(blocks // 16)] for _ in range(2)]
        here = rolled(c, 0)
        for d0 in range(0, blocks, GROUP):
            pieces = []
            for d in range(d0, d0 + GROUP):
                after = rolled(c, d + 1)
                pieces.append(jnp.where(own, here, after))
                here = after
            hank = jnp.concatenate(pieces, axis=0)
            count = -(-(d0 + GROUP) // 16)
            left = []
            for ref in (rev_f, rev_u):
                left.append(
                    jnp.concatenate(
                        [
                            ref[pl.ds(c * pad + blocks - 1 - d, 16 * count), :].astype(bf16)
                            for d in range(d0, d0 + GROUP)
                        ],
                        axis=1,
                    )
                )
            res = jnp.dot(jnp.concatenate(left, axis=0), hank, preferred_element_type=f32)
            for s in range(2):
                for n in range(count):
                    at = (s * count + n) * 16
                    acc[s][n] = acc[s][n] + res[at : at + 16]
        grad_in = jnp.concatenate(acc[0], axis=0)
        grad_h = jnp.concatenate(acc[1], axis=0)
        rows_o[pl.ds(c, blocks, stride=2 * chans), :] = grad_in
        rows_o[pl.ds(c + chans, blocks, stride=2 * chans), :] = grad_h
        kept[pl.ds(pl.multiple_of(c * blocks, blocks), blocks), :] = grad_h.astype(bf16).astype(f32) * fall_ref[pl.ds(c, 1), :]
        return carry

    lax.fori_loop(0, chans, channel, 0, unroll=True)
    spun = jnp.dot(kept[...], wave_ref[...], precision=highest, preferred_element_type=f32)
    spun = spun.reshape(chans, blocks, LANES) * turn_ref[...]
    total = jnp.sum(spun, axis=1)
    total = total + pltpu.roll(total, LANES // 2, 1)
    high = total.astype(bf16).astype(f32)
    lanes = lax.broadcasted_iota(jnp.int32, total.shape, 1)
    pair = jnp.where(lanes < LANES // 2, high, total - high).astype(bf16)
    for t in range(blocks):
        out_ref[t, : 2 * chans, :] = rows_o[2 * chans * t : 2 * chans * (t + 1), :].astype(bf16)
        out_ref[t, 2 * chans :, :] = pair


def run_slab(got, filt, turn, wave, fall, flip, interpret=False):
    blocks, rows, _ = got.shape
    chans = rows // 2
    f32 = jnp.float32
    return pl.pallas_call(
        slab_kernel,
        out_shape=jax.ShapeDtypeStruct((blocks, 3 * chans, LANES), jnp.bfloat16),
        scratch_shapes=[
            pltpu.VMEM((chans * 2 * blocks, LANES), f32),
            pltpu.VMEM((chans * 2 * blocks, LANES), f32),
            pltpu.VMEM((chans * (blocks + 8), LANES), f32),
            pltpu.VMEM((2 * chans * blocks, LANES), f32),
            pltpu.VMEM((chans * blocks, LANES), f32),
        ],
        compiler_params=pltpu.CompilerParams(vmem_limit_bytes=32 << 20),
        interpret=interpret,
    )(got, filt, turn, wave, fall, flip)


def filter_tables(weights, rates, frequency, phase_shift, blocks):
    hi = (LANES * jnp.arange(blocks)).astype(jnp.float32)
    lo = jnp.arange(LANES).astype(jnp.float32)
    outer = frequency[None, :] * hi[:, None] + phase_shift[None, :]
    inner = frequency[:, None] * lo[None, :]
    turn = jnp.concatenate([jnp.sin(outer), jnp.cos(outer)], axis=1)
    wave = jnp.concatenate([jnp.cos(inner), jnp.sin(inner)], axis=0)
    turn = jnp.exp(-rates[:, None] * hi[None, :])[:, :, None] * turn[None]
    fall = jnp.exp(-rates[:, None] * lo[None, :])
    both = jnp.concatenate([weights, weights], axis=1)
    mixed = jnp.einsum("ckj,jl->ckl", (turn * both[:, None, :])[:, ::-1], wave[:, ::-1], precision=highest)
    filt = mixed * fall[:, None, ::-1]
    return filt, turn, wave.T, fall


def pack_kernel(u_ref, g_ref, out_ref, both, sems):
    blocks, chans, _ = u_ref.shape
    size = blocks // CHUNKS
    arriving, leaving = [], []
    for i in range(CHUNKS):
        span = pl.ds(i * size, size)
        for s, ref in enumerate((u_ref, g_ref)):
            copy = pltpu.make_async_copy(
                ref.at[span], both.at[span, s * chans : (s + 1) * chans, :], sems.at[2 * i + s]
            )
            copy.start()
            arriving.append(copy)
    for i in range(CHUNKS):
        span = pl.ds(i * size, size)
        arriving[2 * i].wait()
        arriving[2 * i + 1].wait()
        copy = pltpu.make_async_copy(both.at[span], out_ref.at[span], sems.at[2 * CHUNKS + i])
        copy.start()
        leaving.append(copy)
    for copy in leaving:
        copy.wait()


def partial_kernel(home_ref, rows_ref, out_ref):
    groups, rows, lanes = home_ref.shape
    chans = rows // 3
    pair = home_ref[:, 2 * chans :, :].astype(jnp.float32).reshape(groups * chans, lanes)
    sums = jnp.dot(rows_ref[...], pair, precision=highest, preferred_element_type=jnp.float32)
    folded = sums + pltpu.roll(sums, lanes // 2, 1)
    for part in range(out_ref.shape[0]):
        out_ref[part] = folded


def per_device(inputs, grad_out, out_weight, decay_rate, frequency, phase_shift, sketch_matrix):
    groups = lax.axis_size("seq")
    parts = lax.axis_size("chan")
    seq_index = lax.axis_index("seq")
    width_local, tok_len = inputs.shape
    chans = width_local // groups
    order = frequency.shape[0]
    rank = sketch_matrix.shape[1]
    f32 = jnp.float32
    first_row = seq_index * chans
    sent = pl.pallas_call(
        pack_kernel,
        out_shape=jax.ShapeDtypeStruct((groups, 2 * chans, tok_len), inputs.dtype),
        in_specs=[pl.BlockSpec(memory_space=pl.ANY)] * 2,
        out_specs=pl.BlockSpec(memory_space=pl.ANY),
        scratch_shapes=[
            pltpu.VMEM((groups, 2 * chans, tok_len), inputs.dtype),
            pltpu.SemaphoreType.DMA((3 * CHUNKS,)),
        ],
    )(inputs.reshape(groups, chans, tok_len), grad_out.reshape(groups, chans, tok_len))
    got = lax.all_to_all(sent, "seq", split_axis=0, concat_axis=0, tiled=True)
    rates = lax.dynamic_slice_in_dim(decay_rate, first_row, chans, 0)
    weights = lax.dynamic_slice_in_dim(out_weight, first_row, chans, 0)
    filt, turn, wave, fall = filter_tables(weights, rates, frequency, phase_shift, groups)
    flip = jnp.eye(LANES, dtype=jnp.bfloat16)[::-1]
    back = run_slab(got, filt, turn, wave, fall, flip)
    home = lax.all_to_all(back, "seq", split_axis=0, concat_axis=0, tiled=True)
    everyone = pl.pallas_call(partial_kernel, out_shape=jax.ShapeDtypeStruct((parts, rank, LANES), f32))(
        pltpu.with_memory_space_constraint(home, pltpu.VMEM),
        pltpu.with_memory_space_constraint(sketch_matrix.T, pltpu.VMEM),
    )
    gathered = lax.all_to_all(everyone, "chan", split_axis=0, concat_axis=0, tiled=True)
    sketch = jnp.sum(gathered[:, :, :order], axis=0)
    grad_in = home[:, :chans, :].reshape(width_local, tok_len)
    grad_h = home[:, chans : 2 * chans, :].reshape(width_local, tok_len)
    return (grad_in, grad_h, sketch)


def solution(mesh):
    placed = (
        P("chan", "seq"),
        P("chan", "seq"),
        P("chan", None),
        P("chan"),
        P(),
        P(),
        P("chan", None),
    )
    return jax.shard_map(
        per_device,
        mesh=mesh,
        in_specs=placed,
        out_specs=(P("chan", "seq"), P("chan", "seq"), P()),
        check_vma=False,
    )
```

```python
import math

import jax
import jax.numpy as jnp
from jax import lax
from jax.experimental import pallas as pl
from jax.experimental.pallas import tpu as pltpu
from jax.sharding import PartitionSpec as P

LANES = 128
GROUP = 4
CHUNKS = 4

highest = lax.Precision.HIGHEST


def slab_kernel(got_ref, filt_ref, turn_ref, wave_ref, flip_ref, out_ref, even_u, odd_u, wins_u, rows_g, rows_o, kept):
    blocks = got_ref.shape[0]
    chans = filt_ref.shape[0]
    shifts = filt_ref.shape[2]
    half = LANES // 2
    f32, bf16 = jnp.float32, jnp.bfloat16
    pad = even_u.shape[0] // chans
    gpad = rows_g.shape[0] // chans
    left8 = lax.broadcasted_iota(jnp.int32, (chans, LANES), 1) < half
    for c in range(chans):
        even_u[c * pad + blocks : (c + 1) * pad, :] = jnp.zeros((pad - blocks, LANES), f32)
        odd_u[c * pad + blocks : (c + 1) * pad, :] = jnp.zeros((pad - blocks, LANES), f32)
        rows_g[c * gpad + blocks : (c + 1) * gpad, :] = jnp.zeros((gpad - blocks, LANES), f32)
    turned = jnp.dot(got_ref[...].reshape(blocks * 2 * chans, LANES), flip_ref[...], preferred_element_type=f32)
    last = (jnp.zeros((chans, LANES), f32), jnp.zeros((chans, LANES), f32))
    for t in range(blocks):
        rows = turned[2 * chans * t : 2 * chans * t + chans]
        odd_even, even_odd = rows[:, :LANES], rows[:, LANES:]
        at = blocks - 1 - t
        even_u[pl.ds(at, chans, stride=pad), :] = jnp.where(left8, last[1], odd_even)
        odd_u[pl.ds(at, chans, stride=pad), :] = jnp.where(left8, last[0], even_odd)
        last = (odd_even, even_odd)
        rows_g[pl.ds(t, chans, stride=gpad), :] = got_ref[t].astype(f32)[chans:]

    row_id = lax.broadcasted_iota(jnp.int32, (half, LANES), 0)
    lane_id = lax.broadcasted_iota(jnp.int32, (half, LANES), 1)
    own = (lane_id <= row_id + half).astype(bf16) > 0.5
    left = (lane_id < half).astype(bf16) > 0.5

    for c in range(chans):

        def rolled(d):
            if d >= blocks:
                return jnp.zeros((half, LANES), bf16)
            row = jnp.broadcast_to(rows_g[c * gpad + d : c * gpad + d + 1, :], (half, LANES))
            return pltpu.roll(row, half + 1, 1, stride=1, stride_axis=0).astype(bf16)

        for r in range(shifts):
            wins_u[c, 0, r] = even_u[c * pad + 2 * r : c * pad + 2 * r + blocks, :].astype(bf16)
            wins_u[c, 1, r] = odd_u[c * pad + 2 * r : c * pad + 2 * r + blocks, :].astype(bf16)
        acc = [[[None] * (blocks // 16) for _ in range(2)] for _ in range(2)]
        rolls = [rolled(0), rolled(1)]
        here = jnp.where(own, rolls[0], rolls[1])
        for d0 in range(0, blocks, GROUP):
            hank = ([], [])
            for d in range(d0, d0 + GROUP):
                rolls = [rolls[1], rolled(d + 2)]
                after = jnp.where(own, rolls[0], rolls[1])
                hank[0].append(here)
                hank[1].append(jnp.where(left, after, here))
                here = after
            first = (blocks - 2 - d0) // 16
            count = blocks // 16 - first
            for h in range(2):
                pieces = []
                for wins in (filt_ref, wins_u):
                    pieces.append(
                        jnp.concatenate(
                            [
                                wins[c, h, (blocks - 2 - d) % 16 // 2, 16 * first : blocks, :]
                                for d in range(d0, d0 + GROUP, 2)
                            ],
                            axis=1,
                        )
                    )
                res = jnp.dot(
                    jnp.concatenate(pieces, axis=0), jnp.concatenate(hank[h], axis=0), preferred_element_type=f32
                )
                for s in range(2):
                    for n in range(count):
                        part = res[(s * count + n) * 16 : (s * count + n + 1) * 16]
                        acc[h][s][n] = part if acc[h][s][n] is None else acc[h][s][n] + part
        sums = [
            jnp.concatenate(acc[0][s], axis=0) + pltpu.roll(jnp.concatenate(acc[1][s], axis=0), half, 1)
            for s in range(2)
        ]
        rows_o[pl.ds(c, blocks, stride=2 * chans), :] = sums[0]
        rows_o[pl.ds(c + chans, blocks, stride=2 * chans), :] = sums[1]
        kept[c * blocks : (c + 1) * blocks, :] = sums[1].astype(bf16)
    mixes = []
    for c in range(chans):
        spun = jnp.dot(kept[c * blocks : (c + 1) * blocks, :], wave_ref[c], preferred_element_type=f32)
        spun = (spun[:, :LANES] + spun[:, LANES:]) * turn_ref[c]
        mixes.append(jnp.sum(spun, axis=0, keepdims=True))
    total = jnp.concatenate(mixes, axis=0)
    total = total + pltpu.roll(total, half, 1)
    high = total.astype(bf16).astype(f32)
    pair = jnp.where(left8, high, total - high).astype(bf16)
    for t in range(blocks):
        out_ref[t, : 2 * chans, :] = rows_o[2 * chans * t : 2 * chans * (t + 1), :].astype(bf16)
        out_ref[t, 2 * chans :, :] = pair


def run_slab(got, filt, turn, wave, flip, interpret=False):
    blocks, rows, _ = got.shape
    chans = rows // 2
    f32 = jnp.float32
    return pl.pallas_call(
        slab_kernel,
        out_shape=jax.ShapeDtypeStruct((blocks, 3 * chans, LANES), jnp.bfloat16),
        scratch_shapes=[
            pltpu.VMEM((chans * (blocks + 16), LANES), f32),
            pltpu.VMEM((chans * (blocks + 16), LANES), f32),
            pltpu.VMEM(filt.shape, jnp.bfloat16),
            pltpu.VMEM((chans * (blocks + 8), LANES), f32),
            pltpu.VMEM((2 * chans * blocks, LANES), f32),
            pltpu.VMEM((chans * blocks, LANES), jnp.bfloat16),
        ],
        compiler_params=pltpu.CompilerParams(vmem_limit_bytes=40 << 20),
        interpret=interpret,
    )(got, filt, turn, wave, flip)


def half_windows(filt, blocks):
    after = jnp.pad(filt, ((0, 0), (0, 1), (0, 0)))[:, 1:]
    half = LANES // 2
    even = jnp.concatenate([after[:, :, half:], filt[:, :, half:]], axis=2)
    odd = jnp.concatenate([after[:, :, :half], filt[:, :, :half]], axis=2)
    both = jnp.pad(jnp.stack([even, odd], axis=1), ((0, 0), (0, 0), (0, 16), (0, 0)))
    return jnp.stack([both[:, :, r : r + blocks] for r in range(0, 16, 2)], axis=2).astype(jnp.bfloat16)


def flip_table():
    flip = jnp.eye(LANES, dtype=jnp.bfloat16)[::-1]
    return jnp.concatenate([flip, jnp.roll(flip, LANES // 2, axis=1)], axis=1)


def filter_tables(weights, rates, frequency, phase_shift, blocks):
    hi = (LANES * jnp.arange(blocks)).astype(jnp.float32)
    lo = jnp.arange(LANES).astype(jnp.float32)
    outer = frequency[None, :] * hi[:, None] + phase_shift[None, :]
    inner = frequency[:, None] * lo[None, :]
    turn = jnp.concatenate([jnp.sin(outer), jnp.cos(outer)], axis=1)
    wave = jnp.concatenate([jnp.cos(inner), jnp.sin(inner)], axis=0)
    turn = jnp.exp(-rates[:, None] * hi[None, :])[:, :, None] * turn[None]
    fall = jnp.exp(-rates[:, None] * lo[None, :])
    both = jnp.concatenate([weights, weights], axis=1)
    mixed = jnp.einsum("ckj,jl->ckl", (turn * both[:, None, :])[:, ::-1], wave[:, ::-1], precision=highest)
    filt = mixed * fall[:, None, ::-1]
    spin = fall[:, :, None] * wave.T[None]
    high = lax.reduce_precision(spin, 8, 7)
    spin = jnp.concatenate([high, spin - high], axis=2).astype(jnp.bfloat16)
    return half_windows(filt, blocks), turn, spin


def pack_kernel(u_ref, g_ref, out_ref, both, sems):
    blocks, chans, _ = u_ref.shape
    size = blocks // CHUNKS
    arriving, leaving = [], []
    for i in range(CHUNKS):
        span = pl.ds(i * size, size)
        for s, ref in enumerate((u_ref, g_ref)):
            copy = pltpu.make_async_copy(
                ref.at[span], both.at[span, s * chans : (s + 1) * chans, :], sems.at[2 * i + s]
            )
            copy.start()
            arriving.append(copy)
    for i in range(CHUNKS):
        span = pl.ds(i * size, size)
        arriving[2 * i].wait()
        arriving[2 * i + 1].wait()
        copy = pltpu.make_async_copy(both.at[span], out_ref.at[span], sems.at[2 * CHUNKS + i])
        copy.start()
        leaving.append(copy)
    for copy in leaving:
        copy.wait()


def partial_kernel(home_ref, rows_ref, out_ref):
    groups, rows, lanes = home_ref.shape
    chans = rows // 3
    pair = home_ref[:, 2 * chans :, :].astype(jnp.float32).reshape(groups * chans, lanes)
    sums = jnp.dot(rows_ref[...], pair, precision=highest, preferred_element_type=jnp.float32)
    folded = sums + pltpu.roll(sums, lanes // 2, 1)
    for part in range(out_ref.shape[0]):
        out_ref[part] = folded


def per_device(inputs, grad_out, out_weight, decay_rate, frequency, phase_shift, sketch_matrix):
    groups = lax.axis_size("seq")
    parts = lax.axis_size("chan")
    seq_index = lax.axis_index("seq")
    width_local, tok_len = inputs.shape
    chans = width_local // groups
    order = frequency.shape[0]
    rank = sketch_matrix.shape[1]
    f32 = jnp.float32
    first_row = seq_index * chans
    sent = pl.pallas_call(
        pack_kernel,
        out_shape=jax.ShapeDtypeStruct((groups, 2 * chans, tok_len), inputs.dtype),
        in_specs=[pl.BlockSpec(memory_space=pl.ANY)] * 2,
        out_specs=pl.BlockSpec(memory_space=pl.ANY),
        scratch_shapes=[
            pltpu.VMEM((groups, 2 * chans, tok_len), inputs.dtype),
            pltpu.SemaphoreType.DMA((3 * CHUNKS,)),
        ],
    )(inputs.reshape(groups, chans, tok_len), grad_out.reshape(groups, chans, tok_len))
    got = lax.all_to_all(sent, "seq", split_axis=0, concat_axis=0, tiled=True)
    rates = lax.dynamic_slice_in_dim(decay_rate, first_row, chans, 0)
    weights = lax.dynamic_slice_in_dim(out_weight, first_row, chans, 0)
    filt, turn, wave = filter_tables(weights, rates, frequency, phase_shift, groups)
    flip = flip_table()
    back = run_slab(got, filt, turn, wave, flip)
    home = lax.all_to_all(back, "seq", split_axis=0, concat_axis=0, tiled=True)
    everyone = pl.pallas_call(partial_kernel, out_shape=jax.ShapeDtypeStruct((parts, rank, LANES), f32))(
        pltpu.with_memory_space_constraint(home, pltpu.VMEM),
        pltpu.with_memory_space_constraint(sketch_matrix.T, pltpu.VMEM),
    )
    gathered = lax.all_to_all(everyone, "chan", split_axis=0, concat_axis=0, tiled=True)
    sketch = jnp.sum(gathered[:, :, :order], axis=0)
    grad_in = home[:, :chans, :].reshape(width_local, tok_len)
    grad_h = home[:, chans : 2 * chans, :].reshape(width_local, tok_len)
    return (grad_in, grad_h, sketch)


def solution(mesh):
    placed = (
        P("chan", "seq"),
        P("chan", "seq"),
        P("chan", None),
        P("chan"),
        P(),
        P(),
        P("chan", None),
    )
    return jax.shard_map(
        per_device,
        mesh=mesh,
        in_specs=placed,
        out_specs=(P("chan", "seq"), P("chan", "seq"), P()),
        check_vma=False,
    )
```

```python
import math

import jax
import jax.numpy as jnp
from jax import lax
from jax.experimental import pallas as pl
from jax.experimental.pallas import tpu as pltpu
from jax.sharding import PartitionSpec as P

LANES = 128
GROUP = 4
CHUNKS = 4

highest = lax.Precision.HIGHEST


def slab_kernel(got_ref, filt_ref, turn_ref, wave_ref, flip_ref, out_ref, even_u, odd_u, wins_u, rows_g, rows_o, kept):
    blocks = got_ref.shape[0]
    chans = filt_ref.shape[0]
    shifts = filt_ref.shape[2]
    half = LANES // 2
    f32, bf16 = jnp.float32, jnp.bfloat16
    pad = even_u.shape[0] // chans
    gpad = rows_g.shape[0] // chans
    left8 = lax.broadcasted_iota(jnp.int32, (chans, LANES), 1) < half
    for c in range(chans):
        even_u[c * pad + blocks : (c + 1) * pad, :] = jnp.zeros((pad - blocks, LANES), f32)
        odd_u[c * pad + blocks : (c + 1) * pad, :] = jnp.zeros((pad - blocks, LANES), f32)
        rows_g[c * gpad + blocks : (c + 1) * gpad, :] = jnp.zeros((gpad - blocks, LANES), f32)
    turned = jnp.dot(got_ref[...].reshape(blocks * 2 * chans, LANES), flip_ref[...], preferred_element_type=f32)
    last = (jnp.zeros((chans, LANES), f32), jnp.zeros((chans, LANES), f32))
    for t in range(blocks):
        rows = turned[2 * chans * t : 2 * chans * t + chans]
        odd_even, even_odd = rows[:, :LANES], rows[:, LANES:]
        at = blocks - 1 - t
        even_u[pl.ds(at, chans, stride=pad), :] = jnp.where(left8, last[1], odd_even)
        odd_u[pl.ds(at, chans, stride=pad), :] = jnp.where(left8, last[0], even_odd)
        last = (odd_even, even_odd)
        rows_g[pl.ds(t, chans, stride=gpad), :] = got_ref[t].astype(f32)[chans:]

    row_id = lax.broadcasted_iota(jnp.int32, (half, LANES), 0)
    lane_id = lax.broadcasted_iota(jnp.int32, (half, LANES), 1)
    own = (lane_id <= row_id + half).astype(bf16) > 0.5
    left = (lane_id < half).astype(bf16) > 0.5

    for c in range(chans):

        def rolled(d):
            if d >= blocks:
                return jnp.zeros((half, LANES), bf16)
            row = jnp.broadcast_to(rows_g[c * gpad + d : c * gpad + d + 1, :], (half, LANES))
            return pltpu.roll(row, half + 1, 1, stride=1, stride_axis=0).astype(bf16)

        for r in range(shifts):
            wins_u[c, 0, r] = even_u[c * pad + 2 * r : c * pad + 2 * r + blocks, :].astype(bf16)
            wins_u[c, 1, r] = odd_u[c * pad + 2 * r : c * pad + 2 * r + blocks, :].astype(bf16)
        acc = [[[None] * (blocks // 16) for _ in range(2)] for _ in range(2)]
        rolls = [rolled(0), rolled(1)]
        here = jnp.where(own, rolls[0], rolls[1])
        for d0 in range(0, blocks, GROUP):
            hank = ([], [])
            for d in range(d0, d0 + GROUP):
                rolls = [rolls[1], rolled(d + 2)]
                after = jnp.where(own, rolls[0], rolls[1])
                hank[0].append(here)
                hank[1].append(jnp.where(left, after, here))
                here = after
            first = (blocks - 2 - d0) // 16
            count = blocks // 16 - first
            for h in range(2):
                pieces = []
                for wins in (filt_ref, wins_u):
                    pieces.append(
                        jnp.concatenate(
                            [
                                wins[c, h, (blocks - 2 - d) % 16 // 2, 16 * first : blocks, :]
                                for d in range(d0, d0 + GROUP, 2)
                            ],
                            axis=1,
                        )
                    )
                res = jnp.dot(
                    jnp.concatenate(pieces, axis=0), jnp.concatenate(hank[h], axis=0), preferred_element_type=f32
                )
                for s in range(2):
                    for n in range(count):
                        part = res[(s * count + n) * 16 : (s * count + n + 1) * 16]
                        acc[h][s][n] = part if acc[h][s][n] is None else acc[h][s][n] + part
        sums = [
            jnp.concatenate(acc[0][s], axis=0) + pltpu.roll(jnp.concatenate(acc[1][s], axis=0), half, 1)
            for s in range(2)
        ]
        rows_o[pl.ds(c, blocks, stride=2 * chans), :] = sums[0]
        rows_o[pl.ds(c + chans, blocks, stride=2 * chans), :] = sums[1]
        kept[c * blocks : (c + 1) * blocks, :] = sums[1].astype(bf16)
    mixes = []
    for c in range(chans):
        spun = jnp.dot(kept[c * blocks : (c + 1) * blocks, :], wave_ref[c], preferred_element_type=f32)
        spun = (spun[:, :LANES] + spun[:, LANES:]) * turn_ref[c]
        mixes.append(jnp.sum(spun, axis=0, keepdims=True))
    total = jnp.concatenate(mixes, axis=0)
    total = total + pltpu.roll(total, half, 1)
    high = total.astype(bf16).astype(f32)
    pair = jnp.where(left8, high, total - high).astype(bf16)
    for t in range(blocks):
        out_ref[t, : 2 * chans, :] = rows_o[2 * chans * t : 2 * chans * (t + 1), :].astype(bf16)
        out_ref[t, 2 * chans :, :] = pair


def run_slab(got, filt, turn, wave, flip, interpret=False):
    blocks, rows, _ = got.shape
    chans = rows // 2
    f32 = jnp.float32
    return pl.pallas_call(
        slab_kernel,
        out_shape=jax.ShapeDtypeStruct((blocks, 3 * chans, LANES), jnp.bfloat16),
        scratch_shapes=[
            pltpu.VMEM((chans * (blocks + 16), LANES), f32),
            pltpu.VMEM((chans * (blocks + 16), LANES), f32),
            pltpu.VMEM(filt.shape, jnp.bfloat16),
            pltpu.VMEM((chans * (blocks + 8), LANES), f32),
            pltpu.VMEM((2 * chans * blocks, LANES), f32),
            pltpu.VMEM((chans * blocks, LANES), jnp.bfloat16),
        ],
        compiler_params=pltpu.CompilerParams(vmem_limit_bytes=40 << 20),
        interpret=interpret,
    )(got, filt, turn, wave, flip)


def filter_kernel(
    turn_ref, wave_ref, rise_ref, fall_ref, both_ref, filt_ref, mix_ref, spin_ref, flip_ref, rows, even, odd
):
    blocks = turn_ref.shape[1]
    chans = both_ref.shape[1]
    shifts = filt_ref.shape[2]
    pad = rows.shape[0] // chans
    half = LANES // 2
    f32, bf16 = jnp.float32, jnp.bfloat16
    left = lax.broadcasted_iota(jnp.int32, (blocks, LANES), 1) < half
    mixed = []
    for c in range(chans):
        mix_ref[c] = turn_ref[0] * rise_ref[0, :, c : c + 1]
        mixed.append(turn_ref[1] * rise_ref[1, :, c : c + 1] * both_ref[0, c : c + 1, :])
        spin = wave_ref[0] * fall_ref[:, c : c + 1]
        high = spin.astype(bf16)
        spin_ref[c, :, :LANES] = high
        spin_ref[c, :, LANES:] = (spin - high.astype(f32)).astype(bf16)
    filt = jnp.dot(jnp.concatenate(mixed, axis=0), wave_ref[1], precision=highest, preferred_element_type=f32)
    blank = jnp.zeros((pad - blocks, LANES), f32)
    for c in range(chans):
        own = filt[c * blocks : (c + 1) * blocks] * both_ref[1, c : c + 1, :]
        rows[c * pad : c * pad + blocks, :] = own
        rows[c * pad + blocks : (c + 1) * pad, :] = blank
        after = rows[c * pad + 1 : c * pad + 1 + blocks, :]
        even[c * pad : c * pad + blocks, :] = jnp.where(left, pltpu.roll(after, half, 1), own)
        odd[c * pad : c * pad + blocks, :] = jnp.where(left, after, pltpu.roll(own, half, 1))
        even[c * pad + blocks : (c + 1) * pad, :] = blank
        odd[c * pad + blocks : (c + 1) * pad, :] = blank
        for r in range(shifts):
            filt_ref[c, 0, r] = even[c * pad + 2 * r : c * pad + 2 * r + blocks, :].astype(bf16)
            filt_ref[c, 1, r] = odd[c * pad + 2 * r : c * pad + 2 * r + blocks, :].astype(bf16)
    ends = lax.broadcasted_iota(jnp.int32, (LANES, 2 * LANES), 0) + lax.broadcasted_iota(
        jnp.int32, (LANES, 2 * LANES), 1
    )
    lane = lax.broadcasted_iota(jnp.int32, (LANES, 2 * LANES), 1)
    turned = (ends == LANES + half - 1) | (ends == 2 * LANES + half - 1)
    flip_ref[...] = jnp.where(lane < LANES, jnp.where(ends == LANES - 1, 1.0, 0.0), jnp.where(turned, 1.0, 0.0)).astype(bf16)


def filter_tables(weights, rates, frequency, phase_shift, blocks, interpret=False):
    f32, bf16 = jnp.float32, jnp.bfloat16
    chans = rates.shape[0]
    hi = (LANES * jnp.arange(blocks)).astype(f32)
    lo = jnp.arange(LANES).astype(f32)
    twice = jnp.concatenate([frequency, frequency])
    quarter = jnp.arange(2 * frequency.shape[0]) < frequency.shape[0]
    hi = jnp.stack([hi, hi[::-1]])
    outer = twice[None, None, :] * hi[:, :, None] + jnp.concatenate([phase_shift, phase_shift])[None, None, :]
    turn = jnp.where(quarter, jnp.sin(outer), jnp.cos(outer))
    inner = twice[None, :] * lo[:, None]
    plain = jnp.where(quarter, jnp.cos(inner), jnp.sin(inner))
    inner = twice[:, None] * lo[None, ::-1]
    wave = jnp.stack([plain, jnp.where(quarter[:, None], jnp.cos(inner), jnp.sin(inner))])
    rise = jnp.exp(-rates[None, None, :] * hi[:, :, None])
    fall = jnp.exp(-rates[None, :] * lo[:, None])
    both = jnp.stack([jnp.concatenate([weights, weights], axis=1), jnp.exp(-rates[:, None] * lo[None, ::-1])])
    return pl.pallas_call(
        filter_kernel,
        out_shape=(
            jax.ShapeDtypeStruct((chans, 2, 8, blocks, LANES), bf16),
            jax.ShapeDtypeStruct((chans, blocks, LANES), f32),
            jax.ShapeDtypeStruct((chans, LANES, 2 * LANES), bf16),
            jax.ShapeDtypeStruct((LANES, 2 * LANES), bf16),
        ),
        scratch_shapes=[pltpu.VMEM((chans * (blocks + 16), LANES), f32)] * 3,
        compiler_params=pltpu.CompilerParams(vmem_limit_bytes=32 << 20),
        interpret=interpret,
    )(turn, wave, rise, fall, both)


def pack_kernel(u_ref, g_ref, out_ref, both, sems):
    blocks, chans, _ = u_ref.shape
    size = blocks // CHUNKS
    arriving, leaving = [], []
    for i in range(CHUNKS):
        span = pl.ds(i * size, size)
        for s, ref in enumerate((u_ref, g_ref)):
            copy = pltpu.make_async_copy(
                ref.at[span], both.at[span, s * chans : (s + 1) * chans, :], sems.at[2 * i + s]
            )
            copy.start()
            arriving.append(copy)
    for i in range(CHUNKS):
        span = pl.ds(i * size, size)
        arriving[2 * i].wait()
        arriving[2 * i + 1].wait()
        copy = pltpu.make_async_copy(both.at[span], out_ref.at[span], sems.at[2 * CHUNKS + i])
        copy.start()
        leaving.append(copy)
    for copy in leaving:
        copy.wait()


def partial_kernel(home_ref, rows_ref, out_ref):
    groups, rows, lanes = home_ref.shape
    chans = rows // 3
    pair = home_ref[:, 2 * chans :, :].astype(jnp.float32).reshape(groups * chans, lanes)
    sums = jnp.dot(rows_ref[...], pair, precision=highest, preferred_element_type=jnp.float32)
    folded = sums + pltpu.roll(sums, lanes // 2, 1)
    for part in range(out_ref.shape[0]):
        out_ref[part] = folded


def per_device(inputs, grad_out, out_weight, decay_rate, frequency, phase_shift, sketch_matrix):
    groups = lax.axis_size("seq")
    parts = lax.axis_size("chan")
    seq_index = lax.axis_index("seq")
    width_local, tok_len = inputs.shape
    chans = width_local // groups
    order = frequency.shape[0]
    rank = sketch_matrix.shape[1]
    f32 = jnp.float32
    first_row = seq_index * chans
    sent = pl.pallas_call(
        pack_kernel,
        out_shape=jax.ShapeDtypeStruct((groups, 2 * chans, tok_len), inputs.dtype),
        in_specs=[pl.BlockSpec(memory_space=pl.ANY)] * 2,
        out_specs=pl.BlockSpec(memory_space=pl.ANY),
        scratch_shapes=[
            pltpu.VMEM((groups, 2 * chans, tok_len), inputs.dtype),
            pltpu.SemaphoreType.DMA((3 * CHUNKS,)),
        ],
    )(inputs.reshape(groups, chans, tok_len), grad_out.reshape(groups, chans, tok_len))
    got = lax.all_to_all(sent, "seq", split_axis=0, concat_axis=0, tiled=True)
    rates = lax.dynamic_slice_in_dim(decay_rate, first_row, chans, 0)
    weights = lax.dynamic_slice_in_dim(out_weight, first_row, chans, 0)
    filt, turn, wave, flip = filter_tables(weights, rates, frequency, phase_shift, groups)
    back = run_slab(got, filt, turn, wave, flip)
    home = lax.all_to_all(back, "seq", split_axis=0, concat_axis=0, tiled=True)
    everyone = pl.pallas_call(partial_kernel, out_shape=jax.ShapeDtypeStruct((parts, rank, LANES), f32))(
        pltpu.with_memory_space_constraint(home, pltpu.VMEM),
        pltpu.with_memory_space_constraint(sketch_matrix.T, pltpu.VMEM),
    )
    gathered = lax.all_to_all(everyone, "chan", split_axis=0, concat_axis=0, tiled=True)
    sketch = jnp.sum(gathered[:, :, :order], axis=0)
    grad_in = home[:, :chans, :].reshape(width_local, tok_len)
    grad_h = home[:, chans : 2 * chans, :].reshape(width_local, tok_len)
    return (grad_in, grad_h, sketch)


def solution(mesh):
    placed = (
        P("chan", "seq"),
        P("chan", "seq"),
        P("chan", None),
        P("chan"),
        P(),
        P(),
        P("chan", None),
    )
    return jax.shard_map(
        per_device,
        mesh=mesh,
        in_specs=placed,
        out_specs=(P("chan", "seq"), P("chan", "seq"), P()),
        check_vma=False,
    )
```

```python
import math

import jax
import jax.numpy as jnp
from jax import lax
from jax.experimental import pallas as pl
from jax.experimental.pallas import tpu as pltpu
from jax.sharding import PartitionSpec as P

LANES = 128
GROUP = 4
CHUNKS = 4

highest = lax.Precision.HIGHEST


def slab_kernel(got_ref, filt_ref, turn_ref, wave_ref, flip_ref, out_ref, even_u, odd_u, wins_u, rows_g, rows_o, kept):
    blocks = got_ref.shape[0]
    chans = filt_ref.shape[0]
    shifts = filt_ref.shape[2]
    half = LANES // 2
    f32, bf16 = jnp.float32, jnp.bfloat16
    pad = even_u.shape[0] // chans
    gpad = rows_g.shape[0] // chans
    left8 = lax.broadcasted_iota(jnp.int32, (chans, LANES), 1) < half
    for c in range(chans):
        even_u[c * pad + blocks : (c + 1) * pad, :] = jnp.zeros((pad - blocks, LANES), f32)
        odd_u[c * pad + blocks : (c + 1) * pad, :] = jnp.zeros((pad - blocks, LANES), f32)
        rows_g[c * gpad + blocks : (c + 1) * gpad, :] = jnp.zeros((gpad - blocks, LANES), f32)
    turned = jnp.dot(got_ref[...].reshape(blocks * 2 * chans, LANES), flip_ref[...], preferred_element_type=f32)
    last = (jnp.zeros((chans, LANES), f32), jnp.zeros((chans, LANES), f32))
    for t in range(blocks):
        rows = turned[2 * chans * t : 2 * chans * t + chans]
        odd_even, even_odd = rows[:, :LANES], rows[:, LANES:]
        at = blocks - 1 - t
        even_u[pl.ds(at, chans, stride=pad), :] = jnp.where(left8, last[1], odd_even)
        odd_u[pl.ds(at, chans, stride=pad), :] = jnp.where(left8, last[0], even_odd)
        last = (odd_even, even_odd)
        rows_g[pl.ds(t, chans, stride=gpad), :] = got_ref[t].astype(f32)[chans:]

    row_id = lax.broadcasted_iota(jnp.int32, (half, LANES), 0)
    lane_id = lax.broadcasted_iota(jnp.int32, (half, LANES), 1)
    own = (lane_id <= row_id + half).astype(bf16) > 0.5
    left = (lane_id < half).astype(bf16) > 0.5

    for c in range(chans):

        def rolled(d):
            if d >= blocks:
                return jnp.zeros((half, LANES), bf16)
            row = jnp.broadcast_to(rows_g[c * gpad + d : c * gpad + d + 1, :], (half, LANES))
            return pltpu.roll(row, half + 1, 1, stride=1, stride_axis=0).astype(bf16)

        for r in range(shifts):
            wins_u[c, 0, r] = even_u[c * pad + 2 * r : c * pad + 2 * r + blocks, :].astype(bf16)
            wins_u[c, 1, r] = odd_u[c * pad + 2 * r : c * pad + 2 * r + blocks, :].astype(bf16)
        acc = [[[None] * (blocks // 16) for _ in range(2)] for _ in range(2)]
        rolls = [rolled(0), rolled(1)]
        here = jnp.where(own, rolls[0], rolls[1])
        for d0 in range(0, blocks, GROUP):
            hank = ([], [])
            for d in range(d0, d0 + GROUP):
                rolls = [rolls[1], rolled(d + 2)]
                after = jnp.where(own, rolls[0], rolls[1])
                hank[0].append(here)
                hank[1].append(jnp.where(left, after, here))
                here = after
            first = (blocks - 2 - d0) // 16
            count = blocks // 16 - first
            for h in range(2):
                pieces = []
                for wins in (filt_ref, wins_u):
                    pieces.append(
                        jnp.concatenate(
                            [
                                wins[c, h, (blocks - 2 - d) % 16 // 2, 16 * first : blocks, :]
                                for d in range(d0, d0 + GROUP, 2)
                            ],
                            axis=1,
                        )
                    )
                res = jnp.dot(
                    jnp.concatenate(pieces, axis=0), jnp.concatenate(hank[h], axis=0), preferred_element_type=f32
                )
                for s in range(2):
                    for n in range(count):
                        part = res[(s * count + n) * 16 : (s * count + n + 1) * 16]
                        acc[h][s][n] = part if acc[h][s][n] is None else acc[h][s][n] + part
        sums = [
            jnp.concatenate(acc[0][s], axis=0) + pltpu.roll(jnp.concatenate(acc[1][s], axis=0), half, 1)
            for s in range(2)
        ]
        rows_o[pl.ds(c, blocks, stride=2 * chans), :] = sums[0]
        rows_o[pl.ds(c + chans, blocks, stride=2 * chans), :] = sums[1]
        kept[c * blocks : (c + 1) * blocks, :] = sums[1].astype(bf16)
    mixes = []
    for c in range(chans):
        spun = jnp.dot(kept[c * blocks : (c + 1) * blocks, :], wave_ref[c], preferred_element_type=f32)
        spun = (spun[:, :LANES] + spun[:, LANES:]) * turn_ref[c]
        mixes.append(jnp.sum(spun, axis=0, keepdims=True))
    total = jnp.concatenate(mixes, axis=0)
    total = total + pltpu.roll(total, half, 1)
    high = total.astype(bf16).astype(f32)
    pair = jnp.where(left8, high, total - high).astype(bf16)
    for t in range(blocks):
        out_ref[t, : 2 * chans, :] = rows_o[2 * chans * t : 2 * chans * (t + 1), :].astype(bf16)
        out_ref[t, 2 * chans :, :] = pair


def run_slab(got, filt, turn, wave, flip, interpret=False):
    blocks, rows, _ = got.shape
    chans = rows // 2
    f32 = jnp.float32
    return pl.pallas_call(
        slab_kernel,
        out_shape=jax.ShapeDtypeStruct((blocks, 3 * chans, LANES), jnp.bfloat16),
        scratch_shapes=[
            pltpu.VMEM((chans * (blocks + 16), LANES), f32),
            pltpu.VMEM((chans * (blocks + 16), LANES), f32),
            pltpu.VMEM(filt.shape, jnp.bfloat16),
            pltpu.VMEM((chans * (blocks + 8), LANES), f32),
            pltpu.VMEM((2 * chans * blocks, LANES), f32),
            pltpu.VMEM((chans * blocks, LANES), jnp.bfloat16),
        ],
        compiler_params=pltpu.CompilerParams(vmem_limit_bytes=40 << 20),
        interpret=interpret,
    )(got, filt, turn, wave, flip)


def filter_kernel(
    turn_ref, wave_ref, rise_ref, fall_ref, both_ref, filt_ref, mix_ref, spin_ref, flip_ref, rows, even, odd
):
    blocks = turn_ref.shape[1]
    chans = both_ref.shape[1]
    shifts = filt_ref.shape[2]
    pad = rows.shape[0] // chans
    half = LANES // 2
    f32, bf16 = jnp.float32, jnp.bfloat16
    left = lax.broadcasted_iota(jnp.int32, (blocks, LANES), 1) < half
    mixed = []
    for c in range(chans):
        mix_ref[c] = turn_ref[0] * rise_ref[0, :, c : c + 1]
        mixed.append(turn_ref[1] * rise_ref[1, :, c : c + 1] * both_ref[0, c : c + 1, :])
        spin = wave_ref[0] * fall_ref[:, c : c + 1]
        high = spin.astype(bf16)
        spin_ref[c, :, :LANES] = high
        spin_ref[c, :, LANES:] = (spin - high.astype(f32)).astype(bf16)
    filt = jnp.dot(jnp.concatenate(mixed, axis=0), wave_ref[1], precision=highest, preferred_element_type=f32)
    blank = jnp.zeros((pad - blocks, LANES), f32)
    for c in range(chans):
        own = filt[c * blocks : (c + 1) * blocks] * both_ref[1, c : c + 1, :]
        rows[c * pad : c * pad + blocks, :] = own
        rows[c * pad + blocks : (c + 1) * pad, :] = blank
        after = rows[c * pad + 1 : c * pad + 1 + blocks, :]
        even[c * pad : c * pad + blocks, :] = jnp.where(left, pltpu.roll(after, half, 1), own)
        odd[c * pad : c * pad + blocks, :] = jnp.where(left, after, pltpu.roll(own, half, 1))
        even[c * pad + blocks : (c + 1) * pad, :] = blank
        odd[c * pad + blocks : (c + 1) * pad, :] = blank
        for r in range(shifts):
            filt_ref[c, 0, r] = even[c * pad + 2 * r : c * pad + 2 * r + blocks, :].astype(bf16)
            filt_ref[c, 1, r] = odd[c * pad + 2 * r : c * pad + 2 * r + blocks, :].astype(bf16)
    ends = lax.broadcasted_iota(jnp.int32, (LANES, 2 * LANES), 0) + lax.broadcasted_iota(
        jnp.int32, (LANES, 2 * LANES), 1
    )
    lane = lax.broadcasted_iota(jnp.int32, (LANES, 2 * LANES), 1)
    turned = (ends == LANES + half - 1) | (ends == 2 * LANES + half - 1)
    flip_ref[...] = jnp.where(lane < LANES, jnp.where(ends == LANES - 1, 1.0, 0.0), jnp.where(turned, 1.0, 0.0)).astype(bf16)


def filter_tables(weights, rates, frequency, phase_shift, blocks, interpret=False):
    f32, bf16 = jnp.float32, jnp.bfloat16
    chans = rates.shape[0]
    hi = (LANES * jnp.arange(blocks)).astype(f32)
    lo = jnp.arange(LANES).astype(f32)
    twice = jnp.concatenate([frequency, frequency])
    quarter = jnp.arange(2 * frequency.shape[0]) < frequency.shape[0]
    hi = jnp.stack([hi, hi[::-1]])
    outer = twice[None, None, :] * hi[:, :, None] + jnp.concatenate([phase_shift, phase_shift])[None, None, :]
    turn = jnp.where(quarter, jnp.sin(outer), jnp.cos(outer))
    inner = twice[None, :] * lo[:, None]
    plain = jnp.where(quarter, jnp.cos(inner), jnp.sin(inner))
    inner = twice[:, None] * lo[None, ::-1]
    wave = jnp.stack([plain, jnp.where(quarter[:, None], jnp.cos(inner), jnp.sin(inner))])
    rise = jnp.exp(-rates[None, None, :] * hi[:, :, None])
    fall = jnp.exp(-rates[None, :] * lo[:, None])
    both = jnp.stack([jnp.concatenate([weights, weights], axis=1), jnp.exp(-rates[:, None] * lo[None, ::-1])])
    return pl.pallas_call(
        filter_kernel,
        out_shape=(
            jax.ShapeDtypeStruct((chans, 2, 8, blocks, LANES), bf16),
            jax.ShapeDtypeStruct((chans, blocks, LANES), f32),
            jax.ShapeDtypeStruct((chans, LANES, 2 * LANES), bf16),
            jax.ShapeDtypeStruct((LANES, 2 * LANES), bf16),
        ),
        scratch_shapes=[pltpu.VMEM((chans * (blocks + 16), LANES), f32)] * 3,
        compiler_params=pltpu.CompilerParams(vmem_limit_bytes=32 << 20),
        interpret=interpret,
    )(turn, wave, rise, fall, both)


def pack_kernel(u_ref, g_ref, out_ref, both, sems):
    blocks, chans, _ = u_ref.shape
    size = blocks // CHUNKS
    arriving, leaving = [], []
    for i in range(CHUNKS):
        span = pl.ds(i * size, size)
        for s, ref in enumerate((u_ref, g_ref)):
            copy = pltpu.make_async_copy(
                ref.at[span], both.at[span, s * chans : (s + 1) * chans, :], sems.at[2 * i + s]
            )
            copy.start()
            arriving.append(copy)
    for i in range(CHUNKS):
        span = pl.ds(i * size, size)
        arriving[2 * i].wait()
        arriving[2 * i + 1].wait()
        copy = pltpu.make_async_copy(both.at[span], out_ref.at[span], sems.at[2 * CHUNKS + i])
        copy.start()
        leaving.append(copy)
    for copy in leaving:
        copy.wait()


def unpack_kernel(home_ref, rows_ref, in_ref, h_ref, part_ref, sems):
    groups, rows, lanes = home_ref.shape
    chans = rows // 3
    copies = [
        pltpu.make_async_copy(home_ref.at[:, s * chans : (s + 1) * chans, :], ref, sems.at[s])
        for s, ref in enumerate((in_ref, h_ref))
    ]
    for copy in copies:
        copy.start()
    pair = home_ref[:, 2 * chans :, :].astype(jnp.float32).reshape(groups * chans, lanes)
    sums = jnp.dot(rows_ref[...], pair, precision=highest, preferred_element_type=jnp.float32)
    folded = sums + pltpu.roll(sums, lanes // 2, 1)
    for part in range(part_ref.shape[0]):
        part_ref[part] = folded
    for copy in copies:
        copy.wait()


def per_device(inputs, grad_out, out_weight, decay_rate, frequency, phase_shift, sketch_matrix):
    groups = lax.axis_size("seq")
    parts = lax.axis_size("chan")
    seq_index = lax.axis_index("seq")
    width_local, tok_len = inputs.shape
    chans = width_local // groups
    order = frequency.shape[0]
    rank = sketch_matrix.shape[1]
    f32 = jnp.float32
    first_row = seq_index * chans
    sent = pl.pallas_call(
        pack_kernel,
        out_shape=jax.ShapeDtypeStruct((groups, 2 * chans, tok_len), inputs.dtype),
        in_specs=[pl.BlockSpec(memory_space=pl.ANY)] * 2,
        out_specs=pl.BlockSpec(memory_space=pl.ANY),
        scratch_shapes=[
            pltpu.VMEM((groups, 2 * chans, tok_len), inputs.dtype),
            pltpu.SemaphoreType.DMA((3 * CHUNKS,)),
        ],
    )(inputs.reshape(groups, chans, tok_len), grad_out.reshape(groups, chans, tok_len))
    got = lax.all_to_all(sent, "seq", split_axis=0, concat_axis=0, tiled=True)
    rates = lax.dynamic_slice_in_dim(decay_rate, first_row, chans, 0)
    weights = lax.dynamic_slice_in_dim(out_weight, first_row, chans, 0)
    filt, turn, wave, flip = filter_tables(weights, rates, frequency, phase_shift, groups)
    back = run_slab(got, filt, turn, wave, flip)
    home = lax.all_to_all(back, "seq", split_axis=0, concat_axis=0, tiled=True)
    gradient = jax.ShapeDtypeStruct((groups, chans, tok_len), home.dtype)
    grad_in, grad_h, everyone = pl.pallas_call(
        unpack_kernel,
        out_shape=(gradient, gradient, pltpu.VMEM((parts, rank, LANES), f32)),
        out_specs=(
            pl.BlockSpec(memory_space=pl.ANY),
            pl.BlockSpec(memory_space=pl.ANY),
            pl.BlockSpec(memory_space=pltpu.VMEM),
        ),
        scratch_shapes=[pltpu.SemaphoreType.DMA((2,))],
    )(
        pltpu.with_memory_space_constraint(home, pltpu.VMEM),
        pltpu.with_memory_space_constraint(sketch_matrix.T, pltpu.VMEM),
    )
    gathered = lax.all_to_all(everyone, "chan", split_axis=0, concat_axis=0, tiled=True)
    sketch = jnp.sum(gathered[:, :, :order], axis=0)
    return (grad_in.reshape(width_local, tok_len), grad_h.reshape(width_local, tok_len), sketch)


def solution(mesh):
    placed = (
        P("chan", "seq"),
        P("chan", "seq"),
        P("chan", None),
        P("chan"),
        P(),
        P(),
        P("chan", None),
    )
    return jax.shard_map(
        per_device,
        mesh=mesh,
        in_specs=placed,
        out_specs=(P("chan", "seq"), P("chan", "seq"), P()),
        check_vma=False,
    )
```

```python
import math

import jax
import jax.numpy as jnp
from jax import lax
from jax.experimental import pallas as pl
from jax.experimental.pallas import tpu as pltpu
from jax.sharding import PartitionSpec as P

LANES = 128
GROUP = 4
CHUNKS = 4

highest = lax.Precision.HIGHEST


def slab_kernel(got_ref, filt_ref, turn_ref, wave_ref, flip_ref, out_ref, even_u, odd_u, wins_u, rows_g, rows_o, kept):
    blocks = got_ref.shape[0]
    chans = filt_ref.shape[0]
    shifts = filt_ref.shape[2]
    half = LANES // 2
    f32, bf16 = jnp.float32, jnp.bfloat16
    pad = even_u.shape[0] // chans
    gpad = rows_g.shape[0] // chans
    left8 = lax.broadcasted_iota(jnp.int32, (chans, LANES), 1) < half
    for c in range(chans):
        even_u[c * pad + blocks : (c + 1) * pad, :] = jnp.zeros((pad - blocks, LANES), f32)
        odd_u[c * pad + blocks : (c + 1) * pad, :] = jnp.zeros((pad - blocks, LANES), f32)
        rows_g[c * gpad + blocks : (c + 1) * gpad, :] = jnp.zeros((gpad - blocks, LANES), f32)
    both = got_ref[:, :chans, :].astype(f32).reshape(blocks * chans, LANES).astype(bf16)
    turned = jnp.dot(both, flip_ref[...], preferred_element_type=f32)
    last = (jnp.zeros((chans, LANES), f32), jnp.zeros((chans, LANES), f32))
    for t in range(blocks):
        rows = turned[chans * t : chans * (t + 1)]
        odd_even, even_odd = rows[:, :LANES], rows[:, LANES:]
        at = blocks - 1 - t
        even_u[pl.ds(at, chans, stride=pad), :] = jnp.where(left8, last[1], odd_even)
        odd_u[pl.ds(at, chans, stride=pad), :] = jnp.where(left8, last[0], even_odd)
        last = (odd_even, even_odd)
        rows_g[pl.ds(t, chans, stride=gpad), :] = got_ref[t].astype(f32)[chans:]

    row_id = lax.broadcasted_iota(jnp.int32, (half, LANES), 0)
    lane_id = lax.broadcasted_iota(jnp.int32, (half, LANES), 1)
    own = (lane_id <= row_id + half).astype(bf16) > 0.5
    left = (lane_id < half).astype(bf16) > 0.5

    for c in range(chans):

        def rolled(d):
            if d >= blocks:
                return jnp.zeros((half, LANES), bf16)
            row = jnp.broadcast_to(rows_g[c * gpad + d : c * gpad + d + 1, :], (half, LANES))
            return pltpu.roll(row, half + 1, 1, stride=1, stride_axis=0).astype(bf16)

        for r in range(shifts):
            wins_u[c, 0, r] = even_u[c * pad + 2 * r : c * pad + 2 * r + blocks, :].astype(bf16)
            wins_u[c, 1, r] = odd_u[c * pad + 2 * r : c * pad + 2 * r + blocks, :].astype(bf16)
        acc = [[[None] * (blocks // 16) for _ in range(2)] for _ in range(2)]
        rolls = [rolled(0), rolled(1)]
        here = jnp.where(own, rolls[0], rolls[1])
        for d0 in range(0, blocks, GROUP):
            hank = ([], [])
            for d in range(d0, d0 + GROUP):
                rolls = [rolls[1], rolled(d + 2)]
                after = jnp.where(own, rolls[0], rolls[1])
                hank[0].append(here)
                hank[1].append(jnp.where(left, after, here))
                here = after
            first = (blocks - 2 - d0) // 16
            count = blocks // 16 - first
            for h in range(2):
                pieces = []
                for wins in (filt_ref, wins_u):
                    pieces.append(
                        jnp.concatenate(
                            [
                                wins[c, h, (blocks - 2 - d) % 16 // 2, 16 * first : blocks, :]
                                for d in range(d0, d0 + GROUP, 2)
                            ],
                            axis=1,
                        )
                    )
                res = jnp.dot(
                    jnp.concatenate(pieces, axis=0), jnp.concatenate(hank[h], axis=0), preferred_element_type=f32
                )
                for s in range(2):
                    for n in range(count):
                        part = res[(s * count + n) * 16 : (s * count + n + 1) * 16]
                        acc[h][s][n] = part if acc[h][s][n] is None else acc[h][s][n] + part
        sums = [
            jnp.concatenate(acc[0][s], axis=0) + pltpu.roll(jnp.concatenate(acc[1][s], axis=0), half, 1)
            for s in range(2)
        ]
        rows_o[pl.ds(c, blocks, stride=2 * chans), :] = sums[0]
        rows_o[pl.ds(c + chans, blocks, stride=2 * chans), :] = sums[1]
        kept[c * blocks : (c + 1) * blocks, :] = sums[1].astype(bf16)
    mixes = []
    for c in range(chans):
        spun = jnp.dot(kept[c * blocks : (c + 1) * blocks, :], wave_ref[c], preferred_element_type=f32)
        spun = (spun[:, :LANES] + spun[:, LANES:]) * turn_ref[c]
        mixes.append(jnp.sum(spun, axis=0, keepdims=True))
    total = jnp.concatenate(mixes, axis=0)
    total = total + pltpu.roll(total, half, 1)
    high = total.astype(bf16).astype(f32)
    pair = jnp.where(left8, high, total - high).astype(bf16)
    for t in range(blocks):
        out_ref[t, : 2 * chans, :] = rows_o[2 * chans * t : 2 * chans * (t + 1), :].astype(bf16)
        out_ref[t, 2 * chans :, :] = pair


def run_slab(got, filt, turn, wave, flip, interpret=False):
    blocks, rows, _ = got.shape
    chans = rows // 2
    f32 = jnp.float32
    return pl.pallas_call(
        slab_kernel,
        out_shape=jax.ShapeDtypeStruct((blocks, 3 * chans, LANES), jnp.bfloat16),
        scratch_shapes=[
            pltpu.VMEM((chans * (blocks + 16), LANES), f32),
            pltpu.VMEM((chans * (blocks + 16), LANES), f32),
            pltpu.VMEM(filt.shape, jnp.bfloat16),
            pltpu.VMEM((chans * (blocks + 8), LANES), f32),
            pltpu.VMEM((2 * chans * blocks, LANES), f32),
            pltpu.VMEM((chans * blocks, LANES), jnp.bfloat16),
        ],
        compiler_params=pltpu.CompilerParams(vmem_limit_bytes=40 << 20),
        interpret=interpret,
    )(got, filt, turn, wave, flip)


def filter_kernel(
    turn_ref, wave_ref, rise_ref, fall_ref, both_ref, filt_ref, mix_ref, spin_ref, flip_ref, rows, even, odd
):
    blocks = turn_ref.shape[1]
    chans = both_ref.shape[1]
    shifts = filt_ref.shape[2]
    pad = rows.shape[0] // chans
    half = LANES // 2
    f32, bf16 = jnp.float32, jnp.bfloat16
    left = lax.broadcasted_iota(jnp.int32, (blocks, LANES), 1) < half
    mixed = []
    for c in range(chans):
        mix_ref[c] = turn_ref[0] * rise_ref[0, :, c : c + 1]
        mixed.append(turn_ref[1] * rise_ref[1, :, c : c + 1] * both_ref[0, c : c + 1, :])
        spin = wave_ref[0] * fall_ref[:, c : c + 1]
        high = spin.astype(bf16)
        spin_ref[c, :, :LANES] = high
        spin_ref[c, :, LANES:] = (spin - high.astype(f32)).astype(bf16)
    filt = jnp.dot(jnp.concatenate(mixed, axis=0), wave_ref[1], precision=highest, preferred_element_type=f32)
    blank = jnp.zeros((pad - blocks, LANES), f32)
    for c in range(chans):
        own = filt[c * blocks : (c + 1) * blocks] * both_ref[1, c : c + 1, :]
        rows[c * pad : c * pad + blocks, :] = own
        rows[c * pad + blocks : (c + 1) * pad, :] = blank
        after = rows[c * pad + 1 : c * pad + 1 + blocks, :]
        even[c * pad : c * pad + blocks, :] = jnp.where(left, pltpu.roll(after, half, 1), own)
        odd[c * pad : c * pad + blocks, :] = jnp.where(left, after, pltpu.roll(own, half, 1))
        even[c * pad + blocks : (c + 1) * pad, :] = blank
        odd[c * pad + blocks : (c + 1) * pad, :] = blank
        for r in range(shifts):
            filt_ref[c, 0, r] = even[c * pad + 2 * r : c * pad + 2 * r + blocks, :].astype(bf16)
            filt_ref[c, 1, r] = odd[c * pad + 2 * r : c * pad + 2 * r + blocks, :].astype(bf16)
    ends = lax.broadcasted_iota(jnp.int32, (LANES, 2 * LANES), 0) + lax.broadcasted_iota(
        jnp.int32, (LANES, 2 * LANES), 1
    )
    lane = lax.broadcasted_iota(jnp.int32, (LANES, 2 * LANES), 1)
    turned = (ends == LANES + half - 1) | (ends == 2 * LANES + half - 1)
    flip_ref[...] = jnp.where(lane < LANES, jnp.where(ends == LANES - 1, 1.0, 0.0), jnp.where(turned, 1.0, 0.0)).astype(bf16)


def filter_tables(weights, rates, frequency, phase_shift, blocks, interpret=False):
    f32, bf16 = jnp.float32, jnp.bfloat16
    chans = rates.shape[0]
    hi = (LANES * jnp.arange(blocks)).astype(f32)
    lo = jnp.arange(LANES).astype(f32)
    twice = jnp.concatenate([frequency, frequency])
    quarter = jnp.arange(2 * frequency.shape[0]) < frequency.shape[0]
    hi = jnp.stack([hi, hi[::-1]])
    outer = twice[None, None, :] * hi[:, :, None] + jnp.concatenate([phase_shift, phase_shift])[None, None, :]
    turn = jnp.where(quarter, jnp.sin(outer), jnp.cos(outer))
    inner = twice[None, :] * lo[:, None]
    plain = jnp.where(quarter, jnp.cos(inner), jnp.sin(inner))
    inner = twice[:, None] * lo[None, ::-1]
    wave = jnp.stack([plain, jnp.where(quarter[:, None], jnp.cos(inner), jnp.sin(inner))])
    rise = jnp.exp(-rates[None, None, :] * hi[:, :, None])
    fall = jnp.exp(-rates[None, :] * lo[:, None])
    both = jnp.stack([jnp.concatenate([weights, weights], axis=1), jnp.exp(-rates[:, None] * lo[None, ::-1])])
    return pl.pallas_call(
        filter_kernel,
        out_shape=(
            jax.ShapeDtypeStruct((chans, 2, 8, blocks, LANES), bf16),
            jax.ShapeDtypeStruct((chans, blocks, LANES), f32),
            jax.ShapeDtypeStruct((chans, LANES, 2 * LANES), bf16),
            jax.ShapeDtypeStruct((LANES, 2 * LANES), bf16),
        ),
        scratch_shapes=[pltpu.VMEM((chans * (blocks + 16), LANES), f32)] * 3,
        compiler_params=pltpu.CompilerParams(vmem_limit_bytes=32 << 20),
        interpret=interpret,
    )(turn, wave, rise, fall, both)


def pack_kernel(u_ref, g_ref, out_ref, both, sems):
    blocks, chans, _ = u_ref.shape
    size = blocks // CHUNKS
    arriving, leaving = [], []
    for i in range(CHUNKS):
        span = pl.ds(i * size, size)
        for s, ref in enumerate((u_ref, g_ref)):
            copy = pltpu.make_async_copy(
                ref.at[span], both.at[span, s * chans : (s + 1) * chans, :], sems.at[2 * i + s]
            )
            copy.start()
            arriving.append(copy)
    for i in range(CHUNKS):
        span = pl.ds(i * size, size)
        arriving[2 * i].wait()
        arriving[2 * i + 1].wait()
        copy = pltpu.make_async_copy(both.at[span], out_ref.at[span], sems.at[2 * CHUNKS + i])
        copy.start()
        leaving.append(copy)
    for copy in leaving:
        copy.wait()


def unpack_kernel(home_ref, rows_ref, in_ref, h_ref, part_ref, sems):
    groups, rows, lanes = home_ref.shape
    chans = rows // 3
    copies = [
        pltpu.make_async_copy(home_ref.at[:, s * chans : (s + 1) * chans, :], ref, sems.at[s])
        for s, ref in enumerate((in_ref, h_ref))
    ]
    for copy in copies:
        copy.start()
    pair = home_ref[:, 2 * chans :, :].astype(jnp.float32).reshape(groups * chans, lanes).astype(jnp.bfloat16)
    sums = jnp.dot(rows_ref[...], pair, preferred_element_type=jnp.float32)
    rank = part_ref.shape[1]
    sums = sums[:rank] + (sums[rank : 2 * rank] + sums[2 * rank :])
    folded = sums + pltpu.roll(sums, lanes // 2, 1)
    for part in range(part_ref.shape[0]):
        part_ref[part] = folded
    for copy in copies:
        copy.wait()


def three_parts(values):
    high = lax.reduce_precision(values, 8, 7)
    middle = lax.reduce_precision(values - high, 8, 7)
    return jnp.concatenate([high, middle, values - high - middle], axis=0).astype(jnp.bfloat16)


def per_device(inputs, grad_out, out_weight, decay_rate, frequency, phase_shift, sketch_matrix):
    groups = lax.axis_size("seq")
    parts = lax.axis_size("chan")
    seq_index = lax.axis_index("seq")
    width_local, tok_len = inputs.shape
    chans = width_local // groups
    order = frequency.shape[0]
    rank = sketch_matrix.shape[1]
    f32 = jnp.float32
    first_row = seq_index * chans
    sent = pl.pallas_call(
        pack_kernel,
        out_shape=jax.ShapeDtypeStruct((groups, 2 * chans, tok_len), inputs.dtype),
        in_specs=[pl.BlockSpec(memory_space=pl.ANY)] * 2,
        out_specs=pl.BlockSpec(memory_space=pl.ANY),
        scratch_shapes=[
            pltpu.VMEM((groups, 2 * chans, tok_len), inputs.dtype),
            pltpu.SemaphoreType.DMA((3 * CHUNKS,)),
        ],
    )(inputs.reshape(groups, chans, tok_len), grad_out.reshape(groups, chans, tok_len))
    got = lax.all_to_all(sent, "seq", split_axis=0, concat_axis=0, tiled=True)
    rates = lax.dynamic_slice_in_dim(decay_rate, first_row, chans, 0)
    weights = lax.dynamic_slice_in_dim(out_weight, first_row, chans, 0)
    filt, turn, wave, flip = filter_tables(weights, rates, frequency, phase_shift, groups)
    back = run_slab(got, filt, turn, wave, flip)
    home = lax.all_to_all(back, "seq", split_axis=0, concat_axis=0, tiled=True)
    gradient = jax.ShapeDtypeStruct((groups, chans, tok_len), home.dtype)
    grad_in, grad_h, everyone = pl.pallas_call(
        unpack_kernel,
        out_shape=(gradient, gradient, pltpu.VMEM((parts, rank, LANES), f32)),
        out_specs=(
            pl.BlockSpec(memory_space=pl.ANY),
            pl.BlockSpec(memory_space=pl.ANY),
            pl.BlockSpec(memory_space=pltpu.VMEM),
        ),
        scratch_shapes=[pltpu.SemaphoreType.DMA((2,))],
    )(
        pltpu.with_memory_space_constraint(home, pltpu.VMEM),
        pltpu.with_memory_space_constraint(three_parts(sketch_matrix.T), pltpu.VMEM),
    )
    gathered = lax.all_to_all(everyone, "chan", split_axis=0, concat_axis=0, tiled=True)
    sketch = jnp.sum(gathered[:, :, :order], axis=0)
    return (grad_in.reshape(width_local, tok_len), grad_h.reshape(width_local, tok_len), sketch)


def solution(mesh):
    placed = (
        P("chan", "seq"),
        P("chan", "seq"),
        P("chan", None),
        P("chan"),
        P(),
        P(),
        P("chan", None),
    )
    return jax.shard_map(
        per_device,
        mesh=mesh,
        in_specs=placed,
        out_specs=(P("chan", "seq"), P("chan", "seq"), P()),
        check_vma=False,
    )
```

```python
import math

import jax
import jax.numpy as jnp
from jax import lax
from jax.experimental import pallas as pl
from jax.experimental.pallas import tpu as pltpu
from jax.sharding import PartitionSpec as P

LANES = 128
GROUP = 4
CHUNKS = 4

highest = lax.Precision.HIGHEST


def slab_kernel(got_ref, filt_ref, turn_ref, wave_ref, flip_ref, out_ref, even_u, odd_u, wins_u, rows_g, rows_o, kept):
    blocks = got_ref.shape[0]
    chans = filt_ref.shape[0]
    shifts = filt_ref.shape[2]
    half = LANES // 2
    f32, bf16 = jnp.float32, jnp.bfloat16
    pad = even_u.shape[0] // chans
    gpad = rows_g.shape[0] // chans
    left8 = lax.broadcasted_iota(jnp.int32, (chans, LANES), 1) < half
    for c in range(chans):
        even_u[c * pad + blocks : (c + 1) * pad, :] = jnp.zeros((pad - blocks, LANES), f32)
        odd_u[c * pad + blocks : (c + 1) * pad, :] = jnp.zeros((pad - blocks, LANES), f32)
        rows_g[c * gpad + blocks : (c + 1) * gpad, :] = jnp.zeros((gpad - blocks, LANES), f32)
    both = got_ref[:, :chans, :].astype(f32).reshape(blocks * chans, LANES).astype(bf16)
    turned = jnp.dot(both, flip_ref[...], preferred_element_type=f32)
    last = (jnp.zeros((chans, LANES), f32), jnp.zeros((chans, LANES), f32))
    for t in range(blocks):
        rows = turned[chans * t : chans * (t + 1)]
        odd_even, even_odd = rows[:, :LANES], rows[:, LANES:]
        at = blocks - 1 - t
        even_u[pl.ds(at, chans, stride=pad), :] = jnp.where(left8, last[1], odd_even)
        odd_u[pl.ds(at, chans, stride=pad), :] = jnp.where(left8, last[0], even_odd)
        last = (odd_even, even_odd)
        rows_g[pl.ds(t, chans, stride=gpad), :] = got_ref[t].astype(f32)[chans:]

    row_id = lax.broadcasted_iota(jnp.int32, (half, LANES), 0)
    lane_id = lax.broadcasted_iota(jnp.int32, (half, LANES), 1)
    own = (lane_id <= row_id + half).astype(bf16) > 0.5
    left = (lane_id < half).astype(bf16) > 0.5

    for c in range(chans):

        def rolled(d):
            if d >= blocks:
                return jnp.zeros((half, LANES), bf16)
            row = jnp.broadcast_to(rows_g[c * gpad + d : c * gpad + d + 1, :], (half, LANES))
            return pltpu.roll(row, half + 1, 1, stride=1, stride_axis=0).astype(bf16)

        for r in range(shifts):
            wins_u[c, 0, r] = even_u[c * pad + 2 * r : c * pad + 2 * r + blocks, :].astype(bf16)
            wins_u[c, 1, r] = odd_u[c * pad + 2 * r : c * pad + 2 * r + blocks, :].astype(bf16)
        acc = [[[None] * (blocks // 16) for _ in range(2)] for _ in range(2)]
        rolls = [rolled(0), rolled(1)]
        here = jnp.where(own, rolls[0], rolls[1])
        for d0 in range(0, blocks, GROUP):
            hank = ([], [])
            for d in range(d0, d0 + GROUP):
                rolls = [rolls[1], rolled(d + 2)]
                after = jnp.where(own, rolls[0], rolls[1])
                hank[0].append(here)
                hank[1].append(jnp.where(left, after, here))
                here = after
            first = (blocks - 2 - d0) // 16
            count = blocks // 16 - first
            for h in range(2):
                pieces = []
                for wins in (filt_ref, wins_u):
                    pieces.append(
                        jnp.concatenate(
                            [
                                wins[c, h, (blocks - 2 - d) % 16 // 2, 16 * first : blocks, :]
                                for d in range(d0, d0 + GROUP, 2)
                            ],
                            axis=1,
                        )
                    )
                res = jnp.dot(
                    jnp.concatenate(pieces, axis=0), jnp.concatenate(hank[h], axis=0), preferred_element_type=f32
                )
                for s in range(2):
                    for n in range(count):
                        part = res[(s * count + n) * 16 : (s * count + n + 1) * 16]
                        acc[h][s][n] = part if acc[h][s][n] is None else acc[h][s][n] + part
        sums = [
            jnp.concatenate(acc[0][s], axis=0) + pltpu.roll(jnp.concatenate(acc[1][s], axis=0), half, 1)
            for s in range(2)
        ]
        rows_o[pl.ds(c, blocks, stride=2 * chans), :] = sums[0]
        rows_o[pl.ds(c + chans, blocks, stride=2 * chans), :] = sums[1]
        kept[c * blocks : (c + 1) * blocks, :] = sums[1].astype(bf16)
    mixes = []
    for c in range(chans):
        spun = jnp.dot(kept[c * blocks : (c + 1) * blocks, :], wave_ref[c], preferred_element_type=f32)
        spun = (spun[:, :LANES] + spun[:, LANES:]) * turn_ref[c]
        mixes.append(jnp.sum(spun, axis=0, keepdims=True))
    total = jnp.concatenate(mixes, axis=0)
    total = total + pltpu.roll(total, half, 1)
    high = total.astype(bf16).astype(f32)
    pair = jnp.where(left8, high, total - high).astype(bf16)
    for t in range(blocks):
        out_ref[t, : 2 * chans, :] = rows_o[2 * chans * t : 2 * chans * (t + 1), :].astype(bf16)
        out_ref[t, 2 * chans :, :] = pair


def run_slab(got, filt, turn, wave, flip, interpret=False):
    blocks, rows, _ = got.shape
    chans = rows // 2
    f32 = jnp.float32
    return pl.pallas_call(
        slab_kernel,
        out_shape=jax.ShapeDtypeStruct((blocks, 3 * chans, LANES), jnp.bfloat16),
        scratch_shapes=[
            pltpu.VMEM((chans * (blocks + 16), LANES), f32),
            pltpu.VMEM((chans * (blocks + 16), LANES), f32),
            pltpu.VMEM(filt.shape, jnp.bfloat16),
            pltpu.VMEM((chans * (blocks + 8), LANES), f32),
            pltpu.VMEM((2 * chans * blocks, LANES), f32),
            pltpu.VMEM((chans * blocks, LANES), jnp.bfloat16),
        ],
        compiler_params=pltpu.CompilerParams(vmem_limit_bytes=40 << 20),
        interpret=interpret,
    )(got, filt, turn, wave, flip)


def filter_kernel(
    turn_ref, wave_ref, rise_ref, fall_ref, both_ref, sketch_ref,
    filt_ref, mix_ref, spin_ref, flip_ref, parts_ref, rows, even, odd,
):
    blocks = turn_ref.shape[1]
    chans = both_ref.shape[1]
    shifts = filt_ref.shape[2]
    pad = rows.shape[0] // chans
    half = LANES // 2
    f32, bf16 = jnp.float32, jnp.bfloat16
    left = lax.broadcasted_iota(jnp.int32, (blocks, LANES), 1) < half
    rest = sketch_ref[...]
    rank = rest.shape[0]
    for part in range(3):
        piece = rest.astype(bf16)
        parts_ref[part * rank : (part + 1) * rank, :] = piece
        rest = rest - piece.astype(f32)
    mixed = []
    for c in range(chans):
        mix_ref[c] = turn_ref[0] * rise_ref[0, :, c : c + 1]
        mixed.append(turn_ref[1] * rise_ref[1, :, c : c + 1] * both_ref[0, c : c + 1, :])
        spin = wave_ref[0] * fall_ref[:, c : c + 1]
        high = spin.astype(bf16)
        spin_ref[c, :, :LANES] = high
        spin_ref[c, :, LANES:] = (spin - high.astype(f32)).astype(bf16)
    filt = jnp.dot(jnp.concatenate(mixed, axis=0), wave_ref[1], precision=highest, preferred_element_type=f32)
    blank = jnp.zeros((pad - blocks, LANES), f32)
    for c in range(chans):
        own = filt[c * blocks : (c + 1) * blocks] * both_ref[1, c : c + 1, :]
        rows[c * pad : c * pad + blocks, :] = own
        rows[c * pad + blocks : (c + 1) * pad, :] = blank
        after = rows[c * pad + 1 : c * pad + 1 + blocks, :]
        even[c * pad : c * pad + blocks, :] = jnp.where(left, pltpu.roll(after, half, 1), own)
        odd[c * pad : c * pad + blocks, :] = jnp.where(left, after, pltpu.roll(own, half, 1))
        even[c * pad + blocks : (c + 1) * pad, :] = blank
        odd[c * pad + blocks : (c + 1) * pad, :] = blank
        for r in range(shifts):
            filt_ref[c, 0, r] = even[c * pad + 2 * r : c * pad + 2 * r + blocks, :].astype(bf16)
            filt_ref[c, 1, r] = odd[c * pad + 2 * r : c * pad + 2 * r + blocks, :].astype(bf16)
    ends = lax.broadcasted_iota(jnp.int32, (LANES, 2 * LANES), 0) + lax.broadcasted_iota(
        jnp.int32, (LANES, 2 * LANES), 1
    )
    lane = lax.broadcasted_iota(jnp.int32, (LANES, 2 * LANES), 1)
    turned = (ends == LANES + half - 1) | (ends == 2 * LANES + half - 1)
    flip_ref[...] = jnp.where(lane < LANES, jnp.where(ends == LANES - 1, 1.0, 0.0), jnp.where(turned, 1.0, 0.0)).astype(bf16)


def filter_tables(weights, rates, frequency, phase_shift, sketch_rows, blocks, interpret=False):
    f32, bf16 = jnp.float32, jnp.bfloat16
    chans = rates.shape[0]
    hi = (LANES * jnp.arange(blocks)).astype(f32)
    lo = jnp.arange(LANES).astype(f32)
    twice = jnp.concatenate([frequency, frequency])
    quarter = jnp.arange(2 * frequency.shape[0]) < frequency.shape[0]
    hi = jnp.stack([hi, hi[::-1]])
    outer = twice[None, None, :] * hi[:, :, None] + jnp.concatenate([phase_shift, phase_shift])[None, None, :]
    turn = jnp.where(quarter, jnp.sin(outer), jnp.cos(outer))
    inner = twice[None, :] * lo[:, None]
    plain = jnp.where(quarter, jnp.cos(inner), jnp.sin(inner))
    inner = twice[:, None] * lo[None, ::-1]
    wave = jnp.stack([plain, jnp.where(quarter[:, None], jnp.cos(inner), jnp.sin(inner))])
    rise = jnp.exp(-rates[None, None, :] * hi[:, :, None])
    fall = jnp.exp(-rates[None, :] * lo[:, None])
    both = jnp.stack([jnp.concatenate([weights, weights], axis=1), jnp.exp(-rates[:, None] * lo[None, ::-1])])
    return pl.pallas_call(
        filter_kernel,
        out_shape=(
            jax.ShapeDtypeStruct((chans, 2, 8, blocks, LANES), bf16),
            jax.ShapeDtypeStruct((chans, blocks, LANES), f32),
            jax.ShapeDtypeStruct((chans, LANES, 2 * LANES), bf16),
            jax.ShapeDtypeStruct((LANES, 2 * LANES), bf16),
            jax.ShapeDtypeStruct((3 * sketch_rows.shape[0], sketch_rows.shape[1]), bf16),
        ),
        scratch_shapes=[pltpu.VMEM((chans * (blocks + 16), LANES), f32)] * 3,
        compiler_params=pltpu.CompilerParams(vmem_limit_bytes=32 << 20),
        interpret=interpret,
    )(turn, wave, rise, fall, both, sketch_rows)


def pack_kernel(u_ref, g_ref, out_ref, both, sems):
    blocks, chans, _ = u_ref.shape
    size = blocks // CHUNKS
    arriving, leaving = [], []
    for i in range(CHUNKS):
        span = pl.ds(i * size, size)
        for s, ref in enumerate((u_ref, g_ref)):
            copy = pltpu.make_async_copy(
                ref.at[span], both.at[span, s * chans : (s + 1) * chans, :], sems.at[2 * i + s]
            )
            copy.start()
            arriving.append(copy)
    for i in range(CHUNKS):
        span = pl.ds(i * size, size)
        arriving[2 * i].wait()
        arriving[2 * i + 1].wait()
        copy = pltpu.make_async_copy(both.at[span], out_ref.at[span], sems.at[2 * CHUNKS + i])
        copy.start()
        leaving.append(copy)
    for copy in leaving:
        copy.wait()


def unpack_kernel(home_ref, rows_ref, in_ref, h_ref, part_ref, sems):
    groups, rows, lanes = home_ref.shape
    chans = rows // 3
    copies = [
        pltpu.make_async_copy(home_ref.at[:, s * chans : (s + 1) * chans, :], ref, sems.at[s])
        for s, ref in enumerate((in_ref, h_ref))
    ]
    for copy in copies:
        copy.start()
    pair = home_ref[:, 2 * chans :, :].astype(jnp.float32).reshape(groups * chans, lanes).astype(jnp.bfloat16)
    sums = jnp.dot(rows_ref[...], pair, preferred_element_type=jnp.float32)
    rank = part_ref.shape[1]
    sums = sums[:rank] + (sums[rank : 2 * rank] + sums[2 * rank :])
    folded = sums + pltpu.roll(sums, lanes // 2, 1)
    for part in range(part_ref.shape[0]):
        part_ref[part] = folded
    for copy in copies:
        copy.wait()


def per_device(inputs, grad_out, out_weight, decay_rate, frequency, phase_shift, sketch_matrix):
    groups = lax.axis_size("seq")
    parts = lax.axis_size("chan")
    seq_index = lax.axis_index("seq")
    width_local, tok_len = inputs.shape
    chans = width_local // groups
    order = frequency.shape[0]
    rank = sketch_matrix.shape[1]
    f32 = jnp.float32
    first_row = seq_index * chans
    sent = pl.pallas_call(
        pack_kernel,
        out_shape=jax.ShapeDtypeStruct((groups, 2 * chans, tok_len), inputs.dtype),
        in_specs=[pl.BlockSpec(memory_space=pl.ANY)] * 2,
        out_specs=pl.BlockSpec(memory_space=pl.ANY),
        scratch_shapes=[
            pltpu.VMEM((groups, 2 * chans, tok_len), inputs.dtype),
            pltpu.SemaphoreType.DMA((3 * CHUNKS,)),
        ],
    )(inputs.reshape(groups, chans, tok_len), grad_out.reshape(groups, chans, tok_len))
    got = lax.all_to_all(sent, "seq", split_axis=0, concat_axis=0, tiled=True)
    rates = lax.dynamic_slice_in_dim(decay_rate, first_row, chans, 0)
    weights = lax.dynamic_slice_in_dim(out_weight, first_row, chans, 0)
    filt, turn, wave, flip, sketch_parts = filter_tables(
        weights, rates, frequency, phase_shift, sketch_matrix.T, groups
    )
    back = run_slab(got, filt, turn, wave, flip)
    home = lax.all_to_all(back, "seq", split_axis=0, concat_axis=0, tiled=True)
    gradient = jax.ShapeDtypeStruct((groups, chans, tok_len), home.dtype)
    grad_in, grad_h, everyone = pl.pallas_call(
        unpack_kernel,
        out_shape=(gradient, gradient, pltpu.VMEM((parts, rank, LANES), f32)),
        out_specs=(
            pl.BlockSpec(memory_space=pl.ANY),
            pl.BlockSpec(memory_space=pl.ANY),
            pl.BlockSpec(memory_space=pltpu.VMEM),
        ),
        scratch_shapes=[pltpu.SemaphoreType.DMA((2,))],
    )(
        pltpu.with_memory_space_constraint(home, pltpu.VMEM),
        pltpu.with_memory_space_constraint(sketch_parts, pltpu.VMEM),
    )
    gathered = lax.all_to_all(everyone, "chan", split_axis=0, concat_axis=0, tiled=True)
    sketch = jnp.sum(gathered[:, :, :order], axis=0)
    return (grad_in.reshape(width_local, tok_len), grad_h.reshape(width_local, tok_len), sketch)


def solution(mesh):
    placed = (
        P("chan", "seq"),
        P("chan", "seq"),
        P("chan", None),
        P("chan"),
        P(),
        P(),
        P("chan", None),
    )
    return jax.shard_map(
        per_device,
        mesh=mesh,
        in_specs=placed,
        out_specs=(P("chan", "seq"), P("chan", "seq"), P()),
        check_vma=False,
    )
```

```python
import math

import jax
import jax.numpy as jnp
from jax import lax
from jax.experimental import pallas as pl
from jax.experimental.pallas import tpu as pltpu
from jax.sharding import PartitionSpec as P

LANES = 128
GROUP = 8
CHUNKS = 4

highest = lax.Precision.HIGHEST


def slab_kernel(got_ref, filt_ref, turn_ref, wave_ref, flip_ref, out_ref, even_u, odd_u, wins_u, rows_g, rows_o, kept):
    blocks = got_ref.shape[0]
    chans = filt_ref.shape[0]
    shifts = filt_ref.shape[2]
    half = LANES // 2
    f32, bf16 = jnp.float32, jnp.bfloat16
    pad = even_u.shape[0] // chans
    gpad = rows_g.shape[0] // chans
    left8 = lax.broadcasted_iota(jnp.int32, (chans, LANES), 1) < half
    for c in range(chans):
        even_u[c * pad + blocks : (c + 1) * pad, :] = jnp.zeros((pad - blocks, LANES), f32)
        odd_u[c * pad + blocks : (c + 1) * pad, :] = jnp.zeros((pad - blocks, LANES), f32)
        rows_g[c * gpad + blocks : (c + 1) * gpad, :] = jnp.zeros((gpad - blocks, LANES), f32)
    turned = jnp.dot(got_ref[...].reshape(blocks * 2 * chans, LANES), flip_ref[...], preferred_element_type=f32)
    last = (jnp.zeros((chans, LANES), f32), jnp.zeros((chans, LANES), f32))
    for t in range(blocks):
        rows = turned[2 * chans * t : 2 * chans * t + chans]
        odd_even, even_odd = rows[:, :LANES], rows[:, LANES:]
        at = blocks - 1 - t
        even_u[pl.ds(at, chans, stride=pad), :] = jnp.where(left8, last[1], odd_even)
        odd_u[pl.ds(at, chans, stride=pad), :] = jnp.where(left8, last[0], even_odd)
        last = (odd_even, even_odd)
        rows_g[pl.ds(t, chans, stride=gpad), :] = got_ref[t].astype(f32)[chans:]

    row_id = lax.broadcasted_iota(jnp.int32, (half, LANES), 0)
    lane_id = lax.broadcasted_iota(jnp.int32, (half, LANES), 1)
    own = (lane_id <= row_id + half).astype(bf16) > 0.5
    left = (lane_id < half).astype(bf16) > 0.5

    for c in range(chans):

        def rolled(d):
            if d >= blocks:
                return jnp.zeros((half, LANES), bf16)
            row = jnp.broadcast_to(rows_g[c * gpad + d : c * gpad + d + 1, :], (half, LANES))
            return pltpu.roll(row, half + 1, 1, stride=1, stride_axis=0).astype(bf16)

        for r in range(shifts):
            wins_u[c, 0, r] = even_u[c * pad + 2 * r : c * pad + 2 * r + blocks, :].astype(bf16)
            wins_u[c, 1, r] = odd_u[c * pad + 2 * r : c * pad + 2 * r + blocks, :].astype(bf16)
        acc = [[[None] * (blocks // 16) for _ in range(2)] for _ in range(2)]
        rolls = [rolled(0), rolled(1)]
        here = jnp.where(own, rolls[0], rolls[1])
        for d0 in range(0, blocks, GROUP):
            hank = ([], [])
            for d in range(d0, d0 + GROUP):
                rolls = [rolls[1], rolled(d + 2)]
                after = jnp.where(own, rolls[0], rolls[1])
                hank[0].append(here)
                hank[1].append(jnp.where(left, after, here))
                here = after
            first = (blocks - 2 - d0) // 16
            count = blocks // 16 - first
            for h in range(2):
                pieces = []
                for wins in (filt_ref, wins_u):
                    pieces.append(
                        jnp.concatenate(
                            [
                                wins[c, h, (blocks - 2 - d) % 16 // 2, 16 * first : blocks, :]
                                for d in range(d0, d0 + GROUP, 2)
                            ],
                            axis=1,
                        )
                    )
                res = jnp.dot(
                    jnp.concatenate(pieces, axis=0), jnp.concatenate(hank[h], axis=0), preferred_element_type=f32
                )
                for s in range(2):
                    for n in range(count):
                        part = res[(s * count + n) * 16 : (s * count + n + 1) * 16]
                        acc[h][s][n] = part if acc[h][s][n] is None else acc[h][s][n] + part
        sums = [
            jnp.concatenate(acc[0][s], axis=0) + pltpu.roll(jnp.concatenate(acc[1][s], axis=0), half, 1)
            for s in range(2)
        ]
        rows_o[pl.ds(c, blocks, stride=2 * chans), :] = sums[0]
        rows_o[pl.ds(c + chans, blocks, stride=2 * chans), :] = sums[1]
        kept[c * blocks : (c + 1) * blocks, :] = sums[1].astype(bf16)
    mixes = []
    for c in range(chans):
        spun = jnp.dot(kept[c * blocks : (c + 1) * blocks, :], wave_ref[c], preferred_element_type=f32)
        spun = (spun[:, :LANES] + spun[:, LANES:]) * turn_ref[c]
        mixes.append(jnp.sum(spun, axis=0, keepdims=True))
    total = jnp.concatenate(mixes, axis=0)
    total = total + pltpu.roll(total, half, 1)
    high = total.astype(bf16).astype(f32)
    pair = jnp.where(left8, high, total - high).astype(bf16)
    for t in range(blocks):
        out_ref[t, : 2 * chans, :] = rows_o[2 * chans * t : 2 * chans * (t + 1), :].astype(bf16)
        out_ref[t, 2 * chans :, :] = pair


def run_slab(got, filt, turn, wave, flip, interpret=False):
    blocks, rows, _ = got.shape
    chans = rows // 2
    f32 = jnp.float32
    return pl.pallas_call(
        slab_kernel,
        out_shape=jax.ShapeDtypeStruct((blocks, 3 * chans, LANES), jnp.bfloat16),
        scratch_shapes=[
            pltpu.VMEM((chans * (blocks + 16), LANES), f32),
            pltpu.VMEM((chans * (blocks + 16), LANES), f32),
            pltpu.VMEM(filt.shape, jnp.bfloat16),
            pltpu.VMEM((chans * (blocks + 8), LANES), f32),
            pltpu.VMEM((2 * chans * blocks, LANES), f32),
            pltpu.VMEM((chans * blocks, LANES), jnp.bfloat16),
        ],
        compiler_params=pltpu.CompilerParams(vmem_limit_bytes=40 << 20),
        interpret=interpret,
    )(got, filt, turn, wave, flip)


def filter_kernel(
    turn_ref, wave_ref, rise_ref, fall_ref, both_ref, filt_ref, mix_ref, spin_ref, flip_ref, rows, even, odd
):
    blocks = turn_ref.shape[1]
    chans = both_ref.shape[1]
    shifts = filt_ref.shape[2]
    pad = rows.shape[0] // chans
    half = LANES // 2
    f32, bf16 = jnp.float32, jnp.bfloat16
    left = lax.broadcasted_iota(jnp.int32, (blocks, LANES), 1) < half
    mixed = []
    for c in range(chans):
        mix_ref[c] = turn_ref[0] * rise_ref[0, :, c : c + 1]
        mixed.append(turn_ref[1] * rise_ref[1, :, c : c + 1] * both_ref[0, c : c + 1, :])
        spin = wave_ref[0] * fall_ref[:, c : c + 1]
        high = spin.astype(bf16)
        spin_ref[c, :, :LANES] = high
        spin_ref[c, :, LANES:] = (spin - high.astype(f32)).astype(bf16)
    filt = jnp.dot(jnp.concatenate(mixed, axis=0), wave_ref[1], precision=highest, preferred_element_type=f32)
    blank = jnp.zeros((pad - blocks, LANES), f32)
    for c in range(chans):
        own = filt[c * blocks : (c + 1) * blocks] * both_ref[1, c : c + 1, :]
        rows[c * pad : c * pad + blocks, :] = own
        rows[c * pad + blocks : (c + 1) * pad, :] = blank
        after = rows[c * pad + 1 : c * pad + 1 + blocks, :]
        even[c * pad : c * pad + blocks, :] = jnp.where(left, pltpu.roll(after, half, 1), own)
        odd[c * pad : c * pad + blocks, :] = jnp.where(left, after, pltpu.roll(own, half, 1))
        even[c * pad + blocks : (c + 1) * pad, :] = blank
        odd[c * pad + blocks : (c + 1) * pad, :] = blank
        for r in range(shifts):
            filt_ref[c, 0, r] = even[c * pad + 2 * r : c * pad + 2 * r + blocks, :].astype(bf16)
            filt_ref[c, 1, r] = odd[c * pad + 2 * r : c * pad + 2 * r + blocks, :].astype(bf16)
    ends = lax.broadcasted_iota(jnp.int32, (LANES, 2 * LANES), 0) + lax.broadcasted_iota(
        jnp.int32, (LANES, 2 * LANES), 1
    )
    lane = lax.broadcasted_iota(jnp.int32, (LANES, 2 * LANES), 1)
    turned = (ends == LANES + half - 1) | (ends == 2 * LANES + half - 1)
    flip_ref[...] = jnp.where(lane < LANES, jnp.where(ends == LANES - 1, 1.0, 0.0), jnp.where(turned, 1.0, 0.0)).astype(bf16)


def filter_tables(weights, rates, frequency, phase_shift, blocks, interpret=False):
    f32, bf16 = jnp.float32, jnp.bfloat16
    chans = rates.shape[0]
    hi = (LANES * jnp.arange(blocks)).astype(f32)
    lo = jnp.arange(LANES).astype(f32)
    twice = jnp.concatenate([frequency, frequency])
    quarter = jnp.arange(2 * frequency.shape[0]) < frequency.shape[0]
    hi = jnp.stack([hi, hi[::-1]])
    outer = twice[None, None, :] * hi[:, :, None] + jnp.concatenate([phase_shift, phase_shift])[None, None, :]
    turn = jnp.where(quarter, jnp.sin(outer), jnp.cos(outer))
    inner = twice[None, :] * lo[:, None]
    plain = jnp.where(quarter, jnp.cos(inner), jnp.sin(inner))
    inner = twice[:, None] * lo[None, ::-1]
    wave = jnp.stack([plain, jnp.where(quarter[:, None], jnp.cos(inner), jnp.sin(inner))])
    rise = jnp.exp(-rates[None, None, :] * hi[:, :, None])
    fall = jnp.exp(-rates[None, :] * lo[:, None])
    both = jnp.stack([jnp.concatenate([weights, weights], axis=1), jnp.exp(-rates[:, None] * lo[None, ::-1])])
    return pl.pallas_call(
        filter_kernel,
        out_shape=(
            jax.ShapeDtypeStruct((chans, 2, 8, blocks, LANES), bf16),
            jax.ShapeDtypeStruct((chans, blocks, LANES), f32),
            jax.ShapeDtypeStruct((chans, LANES, 2 * LANES), bf16),
            jax.ShapeDtypeStruct((LANES, 2 * LANES), bf16),
        ),
        scratch_shapes=[pltpu.VMEM((chans * (blocks + 16), LANES), f32)] * 3,
        compiler_params=pltpu.CompilerParams(vmem_limit_bytes=32 << 20),
        interpret=interpret,
    )(turn, wave, rise, fall, both)


def pack_kernel(u_ref, g_ref, out_ref, both, sems):
    blocks, chans, _ = u_ref.shape
    size = blocks // CHUNKS
    arriving, leaving = [], []
    for i in range(CHUNKS):
        span = pl.ds(i * size, size)
        for s, ref in enumerate((u_ref, g_ref)):
            copy = pltpu.make_async_copy(
                ref.at[span], both.at[span, s * chans : (s + 1) * chans, :], sems.at[2 * i + s]
            )
            copy.start()
            arriving.append(copy)
    for i in range(CHUNKS):
        span = pl.ds(i * size, size)
        arriving[2 * i].wait()
        arriving[2 * i + 1].wait()
        copy = pltpu.make_async_copy(both.at[span], out_ref.at[span], sems.at[2 * CHUNKS + i])
        copy.start()
        leaving.append(copy)
    for copy in leaving:
        copy.wait()


def unpack_kernel(home_ref, rows_ref, in_ref, h_ref, part_ref, sems):
    groups, rows, lanes = home_ref.shape
    chans = rows // 3
    copies = [
        pltpu.make_async_copy(home_ref.at[:, s * chans : (s + 1) * chans, :], ref, sems.at[s])
        for s, ref in enumerate((in_ref, h_ref))
    ]
    for copy in copies:
        copy.start()
    pair = home_ref[:, 2 * chans :, :].astype(jnp.float32).reshape(groups * chans, lanes)
    sums = jnp.dot(rows_ref[...], pair, precision=highest, preferred_element_type=jnp.float32)
    folded = sums + pltpu.roll(sums, lanes // 2, 1)
    for part in range(part_ref.shape[0]):
        part_ref[part] = folded
    for copy in copies:
        copy.wait()


def per_device(inputs, grad_out, out_weight, decay_rate, frequency, phase_shift, sketch_matrix):
    groups = lax.axis_size("seq")
    parts = lax.axis_size("chan")
    seq_index = lax.axis_index("seq")
    width_local, tok_len = inputs.shape
    chans = width_local // groups
    order = frequency.shape[0]
    rank = sketch_matrix.shape[1]
    f32 = jnp.float32
    first_row = seq_index * chans
    sent = pl.pallas_call(
        pack_kernel,
        out_shape=jax.ShapeDtypeStruct((groups, 2 * chans, tok_len), inputs.dtype),
        in_specs=[pl.BlockSpec(memory_space=pl.ANY)] * 2,
        out_specs=pl.BlockSpec(memory_space=pl.ANY),
        scratch_shapes=[
            pltpu.VMEM((groups, 2 * chans, tok_len), inputs.dtype),
            pltpu.SemaphoreType.DMA((3 * CHUNKS,)),
        ],
    )(inputs.reshape(groups, chans, tok_len), grad_out.reshape(groups, chans, tok_len))
    got = lax.all_to_all(sent, "seq", split_axis=0, concat_axis=0, tiled=True)
    rates = lax.dynamic_slice_in_dim(decay_rate, first_row, chans, 0)
    weights = lax.dynamic_slice_in_dim(out_weight, first_row, chans, 0)
    filt, turn, wave, flip = filter_tables(weights, rates, frequency, phase_shift, groups)
    back = run_slab(got, filt, turn, wave, flip)
    home = lax.all_to_all(back, "seq", split_axis=0, concat_axis=0, tiled=True)
    gradient = jax.ShapeDtypeStruct((groups, chans, tok_len), home.dtype)
    grad_in, grad_h, everyone = pl.pallas_call(
        unpack_kernel,
        out_shape=(gradient, gradient, pltpu.VMEM((parts, rank, LANES), f32)),
        out_specs=(
            pl.BlockSpec(memory_space=pl.ANY),
            pl.BlockSpec(memory_space=pl.ANY),
            pl.BlockSpec(memory_space=pltpu.VMEM),
        ),
        scratch_shapes=[pltpu.SemaphoreType.DMA((2,))],
    )(
        pltpu.with_memory_space_constraint(home, pltpu.VMEM),
        pltpu.with_memory_space_constraint(sketch_matrix.T, pltpu.VMEM),
    )
    gathered = lax.all_to_all(everyone, "chan", split_axis=0, concat_axis=0, tiled=True)
    sketch = jnp.sum(gathered[:, :, :order], axis=0)
    return (grad_in.reshape(width_local, tok_len), grad_h.reshape(width_local, tok_len), sketch)


def solution(mesh):
    placed = (
        P("chan", "seq"),
        P("chan", "seq"),
        P("chan", None),
        P("chan"),
        P(),
        P(),
        P("chan", None),
    )
    return jax.shard_map(
        per_device,
        mesh=mesh,
        in_specs=placed,
        out_specs=(P("chan", "seq"), P("chan", "seq"), P()),
        check_vma=False,
    )
```

```python
import math

import jax
import jax.numpy as jnp
from jax import lax
from jax.experimental import pallas as pl
from jax.experimental.pallas import tpu as pltpu
from jax.sharding import PartitionSpec as P

LANES = 128
GROUP = 4
CHUNKS = 8

highest = lax.Precision.HIGHEST


def slab_kernel(got_ref, filt_ref, turn_ref, wave_ref, flip_ref, out_ref, even_u, odd_u, wins_u, rows_g, rows_o, kept):
    blocks = got_ref.shape[0]
    chans = filt_ref.shape[0]
    shifts = filt_ref.shape[2]
    half = LANES // 2
    f32, bf16 = jnp.float32, jnp.bfloat16
    pad = even_u.shape[0] // chans
    gpad = rows_g.shape[0] // chans
    left8 = lax.broadcasted_iota(jnp.int32, (chans, LANES), 1) < half
    for c in range(chans):
        even_u[c * pad + blocks : (c + 1) * pad, :] = jnp.zeros((pad - blocks, LANES), f32)
        odd_u[c * pad + blocks : (c + 1) * pad, :] = jnp.zeros((pad - blocks, LANES), f32)
        rows_g[c * gpad + blocks : (c + 1) * gpad, :] = jnp.zeros((gpad - blocks, LANES), f32)
    turned = jnp.dot(got_ref[...].reshape(blocks * 2 * chans, LANES), flip_ref[...], preferred_element_type=f32)
    last = (jnp.zeros((chans, LANES), f32), jnp.zeros((chans, LANES), f32))
    for t in range(blocks):
        rows = turned[2 * chans * t : 2 * chans * t + chans]
        odd_even, even_odd = rows[:, :LANES], rows[:, LANES:]
        at = blocks - 1 - t
        even_u[pl.ds(at, chans, stride=pad), :] = jnp.where(left8, last[1], odd_even)
        odd_u[pl.ds(at, chans, stride=pad), :] = jnp.where(left8, last[0], even_odd)
        last = (odd_even, even_odd)
        rows_g[pl.ds(t, chans, stride=gpad), :] = got_ref[t].astype(f32)[chans:]

    row_id = lax.broadcasted_iota(jnp.int32, (half, LANES), 0)
    lane_id = lax.broadcasted_iota(jnp.int32, (half, LANES), 1)
    own = (lane_id <= row_id + half).astype(bf16) > 0.5
    left = (lane_id < half).astype(bf16) > 0.5

    for c in range(chans):

        def rolled(d):
            if d >= blocks:
                return jnp.zeros((half, LANES), bf16)
            row = jnp.broadcast_to(rows_g[c * gpad + d : c * gpad + d + 1, :], (half, LANES))
            return pltpu.roll(row, half + 1, 1, stride=1, stride_axis=0).astype(bf16)

        for r in range(shifts):
            wins_u[c, 0, r] = even_u[c * pad + 2 * r : c * pad + 2 * r + blocks, :].astype(bf16)
            wins_u[c, 1, r] = odd_u[c * pad + 2 * r : c * pad + 2 * r + blocks, :].astype(bf16)
        acc = [[[None] * (blocks // 16) for _ in range(2)] for _ in range(2)]
        rolls = [rolled(0), rolled(1)]
        here = jnp.where(own, rolls[0], rolls[1])
        for d0 in range(0, blocks, GROUP):
            hank = ([], [])
            for d in range(d0, d0 + GROUP):
                rolls = [rolls[1], rolled(d + 2)]
                after = jnp.where(own, rolls[0], rolls[1])
                hank[0].append(here)
                hank[1].append(jnp.where(left, after, here))
                here = after
            first = (blocks - 2 - d0) // 16
            count = blocks // 16 - first
            for h in range(2):
                pieces = []
                for wins in (filt_ref, wins_u):
                    pieces.append(
                        jnp.concatenate(
                            [
                                wins[c, h, (blocks - 2 - d) % 16 // 2, 16 * first : blocks, :]
                                for d in range(d0, d0 + GROUP, 2)
                            ],
                            axis=1,
                        )
                    )
                res = jnp.dot(
                    jnp.concatenate(pieces, axis=0), jnp.concatenate(hank[h], axis=0), preferred_element_type=f32
                )
                for s in range(2):
                    for n in range(count):
                        part = res[(s * count + n) * 16 : (s * count + n + 1) * 16]
                        acc[h][s][n] = part if acc[h][s][n] is None else acc[h][s][n] + part
        sums = [
            jnp.concatenate(acc[0][s], axis=0) + pltpu.roll(jnp.concatenate(acc[1][s], axis=0), half, 1)
            for s in range(2)
        ]
        rows_o[pl.ds(c, blocks, stride=2 * chans), :] = sums[0]
        rows_o[pl.ds(c + chans, blocks, stride=2 * chans), :] = sums[1]
        kept[c * blocks : (c + 1) * blocks, :] = sums[1].astype(bf16)
    mixes = []
    for c in range(chans):
        spun = jnp.dot(kept[c * blocks : (c + 1) * blocks, :], wave_ref[c], preferred_element_type=f32)
        spun = (spun[:, :LANES] + spun[:, LANES:]) * turn_ref[c]
        mixes.append(jnp.sum(spun, axis=0, keepdims=True))
    total = jnp.concatenate(mixes, axis=0)
    total = total + pltpu.roll(total, half, 1)
    high = total.astype(bf16).astype(f32)
    pair = jnp.where(left8, high, total - high).astype(bf16)
    for t in range(blocks):
        out_ref[t, : 2 * chans, :] = rows_o[2 * chans * t : 2 * chans * (t + 1), :].astype(bf16)
        out_ref[t, 2 * chans :, :] = pair


def run_slab(got, filt, turn, wave, flip, interpret=False):
    blocks, rows, _ = got.shape
    chans = rows // 2
    f32 = jnp.float32
    return pl.pallas_call(
        slab_kernel,
        out_shape=jax.ShapeDtypeStruct((blocks, 3 * chans, LANES), jnp.bfloat16),
        scratch_shapes=[
            pltpu.VMEM((chans * (blocks + 16), LANES), f32),
            pltpu.VMEM((chans * (blocks + 16), LANES), f32),
            pltpu.VMEM(filt.shape, jnp.bfloat16),
            pltpu.VMEM((chans * (blocks + 8), LANES), f32),
            pltpu.VMEM((2 * chans * blocks, LANES), f32),
            pltpu.VMEM((chans * blocks, LANES), jnp.bfloat16),
        ],
        compiler_params=pltpu.CompilerParams(vmem_limit_bytes=40 << 20),
        interpret=interpret,
    )(got, filt, turn, wave, flip)


def filter_kernel(
    turn_ref, wave_ref, rise_ref, fall_ref, both_ref, filt_ref, mix_ref, spin_ref, flip_ref, rows, even, odd
):
    blocks = turn_ref.shape[1]
    chans = both_ref.shape[1]
    shifts = filt_ref.shape[2]
    pad = rows.shape[0] // chans
    half = LANES // 2
    f32, bf16 = jnp.float32, jnp.bfloat16
    left = lax.broadcasted_iota(jnp.int32, (blocks, LANES), 1) < half
    mixed = []
    for c in range(chans):
        mix_ref[c] = turn_ref[0] * rise_ref[0, :, c : c + 1]
        mixed.append(turn_ref[1] * rise_ref[1, :, c : c + 1] * both_ref[0, c : c + 1, :])
        spin = wave_ref[0] * fall_ref[:, c : c + 1]
        high = spin.astype(bf16)
        spin_ref[c, :, :LANES] = high
        spin_ref[c, :, LANES:] = (spin - high.astype(f32)).astype(bf16)
    filt = jnp.dot(jnp.concatenate(mixed, axis=0), wave_ref[1], precision=highest, preferred_element_type=f32)
    blank = jnp.zeros((pad - blocks, LANES), f32)
    for c in range(chans):
        own = filt[c * blocks : (c + 1) * blocks] * both_ref[1, c : c + 1, :]
        rows[c * pad : c * pad + blocks, :] = own
        rows[c * pad + blocks : (c + 1) * pad, :] = blank
        after = rows[c * pad + 1 : c * pad + 1 + blocks, :]
        even[c * pad : c * pad + blocks, :] = jnp.where(left, pltpu.roll(after, half, 1), own)
        odd[c * pad : c * pad + blocks, :] = jnp.where(left, after, pltpu.roll(own, half, 1))
        even[c * pad + blocks : (c + 1) * pad, :] = blank
        odd[c * pad + blocks : (c + 1) * pad, :] = blank
        for r in range(shifts):
            filt_ref[c, 0, r] = even[c * pad + 2 * r : c * pad + 2 * r + blocks, :].astype(bf16)
            filt_ref[c, 1, r] = odd[c * pad + 2 * r : c * pad + 2 * r + blocks, :].astype(bf16)
    ends = lax.broadcasted_iota(jnp.int32, (LANES, 2 * LANES), 0) + lax.broadcasted_iota(
        jnp.int32, (LANES, 2 * LANES), 1
    )
    lane = lax.broadcasted_iota(jnp.int32, (LANES, 2 * LANES), 1)
    turned = (ends == LANES + half - 1) | (ends == 2 * LANES + half - 1)
    flip_ref[...] = jnp.where(lane < LANES, jnp.where(ends == LANES - 1, 1.0, 0.0), jnp.where(turned, 1.0, 0.0)).astype(bf16)


def filter_tables(weights, rates, frequency, phase_shift, blocks, interpret=False):
    f32, bf16 = jnp.float32, jnp.bfloat16
    chans = rates.shape[0]
    hi = (LANES * jnp.arange(blocks)).astype(f32)
    lo = jnp.arange(LANES).astype(f32)
    twice = jnp.concatenate([frequency, frequency])
    quarter = jnp.arange(2 * frequency.shape[0]) < frequency.shape[0]
    hi = jnp.stack([hi, hi[::-1]])
    outer = twice[None, None, :] * hi[:, :, None] + jnp.concatenate([phase_shift, phase_shift])[None, None, :]
    turn = jnp.where(quarter, jnp.sin(outer), jnp.cos(outer))
    inner = twice[None, :] * lo[:, None]
    plain = jnp.where(quarter, jnp.cos(inner), jnp.sin(inner))
    inner = twice[:, None] * lo[None, ::-1]
    wave = jnp.stack([plain, jnp.where(quarter[:, None], jnp.cos(inner), jnp.sin(inner))])
    rise = jnp.exp(-rates[None, None, :] * hi[:, :, None])
    fall = jnp.exp(-rates[None, :] * lo[:, None])
    both = jnp.stack([jnp.concatenate([weights, weights], axis=1), jnp.exp(-rates[:, None] * lo[None, ::-1])])
    return pl.pallas_call(
        filter_kernel,
        out_shape=(
            jax.ShapeDtypeStruct((chans, 2, 8, blocks, LANES), bf16),
            jax.ShapeDtypeStruct((chans, blocks, LANES), f32),
            jax.ShapeDtypeStruct((chans, LANES, 2 * LANES), bf16),
            jax.ShapeDtypeStruct((LANES, 2 * LANES), bf16),
        ),
        scratch_shapes=[pltpu.VMEM((chans * (blocks + 16), LANES), f32)] * 3,
        compiler_params=pltpu.CompilerParams(vmem_limit_bytes=32 << 20),
        interpret=interpret,
    )(turn, wave, rise, fall, both)


def pack_kernel(u_ref, g_ref, out_ref, both, sems):
    blocks, chans, _ = u_ref.shape
    size = blocks // CHUNKS
    arriving, leaving = [], []
    for i in range(CHUNKS):
        span = pl.ds(i * size, size)
        for s, ref in enumerate((u_ref, g_ref)):
            copy = pltpu.make_async_copy(
                ref.at[span], both.at[span, s * chans : (s + 1) * chans, :], sems.at[2 * i + s]
            )
            copy.start()
            arriving.append(copy)
    for i in range(CHUNKS):
        span = pl.ds(i * size, size)
        arriving[2 * i].wait()
        arriving[2 * i + 1].wait()
        copy = pltpu.make_async_copy(both.at[span], out_ref.at[span], sems.at[2 * CHUNKS + i])
        copy.start()
        leaving.append(copy)
    for copy in leaving:
        copy.wait()


def unpack_kernel(home_ref, rows_ref, in_ref, h_ref, part_ref, sems):
    groups, rows, lanes = home_ref.shape
    chans = rows // 3
    copies = [
        pltpu.make_async_copy(home_ref.at[:, s * chans : (s + 1) * chans, :], ref, sems.at[s])
        for s, ref in enumerate((in_ref, h_ref))
    ]
    for copy in copies:
        copy.start()
    pair = home_ref[:, 2 * chans :, :].astype(jnp.float32).reshape(groups * chans, lanes)
    sums = jnp.dot(rows_ref[...], pair, precision=highest, preferred_element_type=jnp.float32)
    folded = sums + pltpu.roll(sums, lanes // 2, 1)
    for part in range(part_ref.shape[0]):
        part_ref[part] = folded
    for copy in copies:
        copy.wait()


def per_device(inputs, grad_out, out_weight, decay_rate, frequency, phase_shift, sketch_matrix):
    groups = lax.axis_size("seq")
    parts = lax.axis_size("chan")
    seq_index = lax.axis_index("seq")
    width_local, tok_len = inputs.shape
    chans = width_local // groups
    order = frequency.shape[0]
    rank = sketch_matrix.shape[1]
    f32 = jnp.float32
    first_row = seq_index * chans
    sent = pl.pallas_call(
        pack_kernel,
        out_shape=jax.ShapeDtypeStruct((groups, 2 * chans, tok_len), inputs.dtype),
        in_specs=[pl.BlockSpec(memory_space=pl.ANY)] * 2,
        out_specs=pl.BlockSpec(memory_space=pl.ANY),
        scratch_shapes=[
            pltpu.VMEM((groups, 2 * chans, tok_len), inputs.dtype),
            pltpu.SemaphoreType.DMA((3 * CHUNKS,)),
        ],
    )(inputs.reshape(groups, chans, tok_len), grad_out.reshape(groups, chans, tok_len))
    got = lax.all_to_all(sent, "seq", split_axis=0, concat_axis=0, tiled=True)
    rates = lax.dynamic_slice_in_dim(decay_rate, first_row, chans, 0)
    weights = lax.dynamic_slice_in_dim(out_weight, first_row, chans, 0)
    filt, turn, wave, flip = filter_tables(weights, rates, frequency, phase_shift, groups)
    back = run_slab(got, filt, turn, wave, flip)
    home = lax.all_to_all(back, "seq", split_axis=0, concat_axis=0, tiled=True)
    gradient = jax.ShapeDtypeStruct((groups, chans, tok_len), home.dtype)
    grad_in, grad_h, everyone = pl.pallas_call(
        unpack_kernel,
        out_shape=(gradient, gradient, pltpu.VMEM((parts, rank, LANES), f32)),
        out_specs=(
            pl.BlockSpec(memory_space=pl.ANY),
            pl.BlockSpec(memory_space=pl.ANY),
            pl.BlockSpec(memory_space=pltpu.VMEM),
        ),
        scratch_shapes=[pltpu.SemaphoreType.DMA((2,))],
    )(
        pltpu.with_memory_space_constraint(home, pltpu.VMEM),
        pltpu.with_memory_space_constraint(sketch_matrix.T, pltpu.VMEM),
    )
    gathered = lax.all_to_all(everyone, "chan", split_axis=0, concat_axis=0, tiled=True)
    sketch = jnp.sum(gathered[:, :, :order], axis=0)
    return (grad_in.reshape(width_local, tok_len), grad_h.reshape(width_local, tok_len), sketch)


def solution(mesh):
    placed = (
        P("chan", "seq"),
        P("chan", "seq"),
        P("chan", None),
        P("chan"),
        P(),
        P(),
        P("chan", None),
    )
    return jax.shard_map(
        per_device,
        mesh=mesh,
        in_specs=placed,
        out_specs=(P("chan", "seq"), P("chan", "seq"), P()),
        check_vma=False,
    )
```
